256 devices in a mesh: head: 4 (over x_hi, core), seq: 64 (over y, z, x_lo).
Axes of the slice: x: 4 (x_hi: 2, x_lo: 2; x = x_hi * 2 + x_lo), y: 4, z: 8, core: 2. Of those that a mesh axis runs over, the one named last changes fastest.
Arguments:
- queries: bfloat16 [8192, 128, 128], P('seq', 'head'), may hold values from -8 to 8
- keys: bfloat16 [8192, 8, 128], P('seq', 'head'), may hold values from -8 to 8
- values: bfloat16 [8192, 8, 128], P('seq', 'head'), may hold values from -12 to 12
- feat_q: float32 [128, 128, 64], P('head'), may hold values from -0.5 to 0.5
- key_feature_weights: float32 [8, 128, 64], P('head'), may hold values from -0.5 to 0.5
- doc_start: int32 [8192], P('seq'), may hold values from 0 to 8191, as said below
Outputs:
- teacher_out: bfloat16 [8192, 128, 128], P('seq', 'head')
- student_out: float32 [8192, 128, 128], P('seq', 'head')
- grad_wq: float32 [128, 128, 64], P('head')
- grad_wk: float32 [8, 128, 64], P('head')
The draws below stay inside these ranges and needn't reach their ends.
Inputs may be any that keep to these rules, and one draw needn't show every extreme that they name: doc_start never falls along the sequence, doc_start[t] <= t, doc_start[0] = 0, and all tokens of one document share it; the sequence holds at most 4 documents.
All inputs are finite; a program needn't handle non-finite values.
Results may differ from the reference program's by a relative error of at most 0.0034.
Values may be sent and summed in bfloat16 or wider, within the bound.
A program may use at most 128 MiB of HBM per device.

```python
import math
import jax
import jax.numpy as jnp
from jax import lax

HEAD_SIZE = 128
VALUE_HEADS = 8
QUERY_HEADS = 128
SIGN_FEATURES = 64
SEQUENCE_TOKENS = 8192


def draw_queries(key, part):
    base = jax.random.fold_in(key, 1)
    array_shape = (SEQUENCE_TOKENS, VALUE_HEADS, QUERY_HEADS // VALUE_HEADS, HEAD_SIZE)
    drawn = 1.5 * jnp.clip(jax.random.normal(base, array_shape, jnp.float32), -4.0, 4.0)
    return drawn.reshape(SEQUENCE_TOKENS, QUERY_HEADS, HEAD_SIZE).astype(jnp.bfloat16)


def draw_keys(key, part):
    base = jax.random.fold_in(key, 2)
    array_shape = (SEQUENCE_TOKENS, VALUE_HEADS, HEAD_SIZE)
    drawn = 1.5 * jnp.clip(jax.random.normal(base, array_shape, jnp.float32), -4.0, 4.0)
    return drawn.astype(jnp.bfloat16)


def draw_doc_start(key, part):
    random_cuts = jax.random.randint(jax.random.fold_in(key, 21), (2,), 1, SEQUENCE_TOKENS)
    cuts = jnp.concatenate([random_cuts, jnp.full((1,), SEQUENCE_TOKENS - 1, jnp.int32)]).astype(jnp.int32)
    positions = jnp.arange(SEQUENCE_TOKENS, dtype=jnp.int32)
    candidates = jnp.where(cuts[None, :] <= positions[:, None], cuts[None, :], 0)
    return jnp.max(candidates, axis=1).astype(jnp.int32)


def steps_of(key, shape, pieces, low, largest):
    level, own = 1.0, jax.random.fold_in(key, 6)
    for axis_at, shards_of in pieces:
        heights = jnp.exp(jax.random.uniform(jax.random.fold_in(own, axis_at), (shards_of,), jnp.float32, low / len(pieces), largest / len(pieces)))
        level = level * jnp.repeat(heights, shape[axis_at] // shards_of).reshape([-1 if axis == axis_at else 1 for axis in range(len(shape))])
    return level


def centred(own_key, shape, spread, limit, shards=(), held_as=jnp.bfloat16):
    values = jax.random.normal(own_key, shape, jnp.float32) * spread
    if len(shards) > 0:
        values = steps_of(own_key, shape, shards, -0.22, 0.18) * values
    return jnp.clip(values, min=-limit, max=limit).astype(held_as)


def setup_inputs(seed: int = 0) -> dict:
    seeds = jax.random.split(jax.random.key(seed), 7)
    return {
        "queries": draw_queries(jax.random.fold_in(seeds[6], 71), 0),
        "keys": draw_keys(jax.random.fold_in(seeds[6], 71), 0),
        "values": centred(seeds[2], (SEQUENCE_TOKENS, VALUE_HEADS, HEAD_SIZE), 2.0, 12.0, ((0, 64), (1, 4))),
        "feat_q": centred(seeds[3], (QUERY_HEADS, HEAD_SIZE, SIGN_FEATURES), HEAD_SIZE ** -0.5, 0.5, ((0, 4),), jnp.float32),
        "key_feature_weights": centred(seeds[4], (VALUE_HEADS, HEAD_SIZE, SIGN_FEATURES), HEAD_SIZE ** -0.5, 0.5, ((0, 4),), jnp.float32),
        "doc_start": draw_doc_start(jax.random.fold_in(seeds[6], 71), 0),
    }


def features(inputs, weight):
    projected = jnp.einsum('thd,hdf->thf', inputs.astype(jnp.float32), weight, precision=lax.Precision.HIGHEST)
    return jnp.concatenate([jax.nn.softplus(projected), jax.nn.softplus(-projected)], axis=-1)

def teacher_attention(queries, keys, values, doc_start):
    token_count, head_count, head_width = queries.shape
    key_heads = keys.shape[1]
    group_size = head_count // key_heads
    block_rows = math.gcd(token_count, 512)
    block_count = token_count // block_rows
    positions = jnp.arange(token_count, dtype=jnp.int32)
    scale = 1.0 / math.sqrt(head_width)
    query_blocks = queries.reshape(block_count, block_rows, key_heads, group_size, head_width)

    def one_block(block_index):
        query_block = lax.dynamic_index_in_dim(query_blocks, block_index, 0, keepdims=False)
        query_pos = block_index * block_rows + jnp.arange(block_rows, dtype=jnp.int32)
        starts = lax.dynamic_slice_in_dim(doc_start, block_index * block_rows, block_rows)
        allowed = (positions[None, :] <= query_pos[:, None]) & (positions[None, :] >= starts[:, None])

        def one_head(head_index):
            query_part = lax.dynamic_index_in_dim(query_block, head_index, 1, keepdims=False).astype(jnp.float32)
            key_part = lax.dynamic_index_in_dim(keys, head_index, 1, keepdims=False).astype(jnp.float32)
            value_part = lax.dynamic_index_in_dim(values, head_index, 1, keepdims=False).astype(jnp.float32)
            scores = jnp.einsum('tjd,sd->jts', query_part, key_part) * scale
            masked = jnp.where(allowed[None], scores, -jnp.inf)
            row_top = lax.optimization_barrier(jnp.max(masked, axis=-1, keepdims=True))
            weights = jnp.where(allowed[None], jnp.exp(scores - row_top), 0.0)
            rounded = lax.optimization_barrier(weights.astype(jnp.bfloat16)).astype(jnp.float32)
            numerator = jnp.einsum('jts,sd->tjd', rounded, value_part)
            denominator = lax.optimization_barrier(jnp.sum(weights, axis=-1))
            return numerator / jnp.transpose(denominator)[:, :, None]
        outputs = lax.map(one_head, jnp.arange(key_heads, dtype=jnp.int32))
        return jnp.transpose(outputs, (1, 0, 2, 3)).reshape(block_rows, head_count, head_width)
    outputs = lax.map(one_block, jnp.arange(block_count, dtype=jnp.int32))
    return outputs.reshape(token_count, head_count, head_width).astype(jnp.bfloat16)

def student_attention(feat_q, key_feature_weights, queries, keys, values, doc_start):
    token_count, head_count, head_width = queries.shape
    key_heads = keys.shape[1]
    group_size = head_count // key_heads
    feat_twice = 2 * feat_q.shape[2]
    block_rows = math.gcd(token_count, 512)
    block_count = token_count // block_rows
    offsets = jnp.arange(block_rows, dtype=jnp.int32)
    highest = lax.Precision.HIGHEST

    def step(running, block_index):
        key_state, key_norm, last_start = running
        begin = block_index * block_rows
        query_block = lax.dynamic_slice_in_dim(queries, begin, block_rows)
        key_block = lax.dynamic_slice_in_dim(keys, begin, block_rows)
        value_block = lax.dynamic_slice_in_dim(values, begin, block_rows).astype(jnp.float32)
        starts = lax.dynamic_slice_in_dim(doc_start, begin, block_rows)
        query_feats = features(query_block, feat_q).reshape(block_rows, key_heads, group_size, feat_twice)
        key_feats = features(key_block, key_feature_weights)
        allowed = (offsets[None, :] <= offsets[:, None]) & ((begin + offsets)[None, :] >= starts[:, None])
        similarity = jnp.einsum('tgjf,sgf->gjts', query_feats, key_feats, precision=highest)
        similarity = jnp.where(allowed[None, None], similarity, 0.0)
        query_match = (starts == last_start).astype(jnp.float32)
        numerator = jnp.einsum('gjts,sgd->tgjd', similarity, value_block, precision=highest)
        numerator = numerator + query_match[:, None, None, None] * jnp.einsum('tgjf,gfd->tgjd', query_feats, key_state, precision=highest)
        denominator = jnp.transpose(lax.optimization_barrier(jnp.sum(similarity, axis=-1)), (2, 0, 1))
        denominator = denominator + query_match[:, None, None] * jnp.einsum('tgjf,gf->tgj', query_feats, key_norm, precision=highest)
        outputs = (numerator / denominator[..., None]).reshape(block_rows, head_count, head_width)
        end_start = starts[block_rows - 1]
        keep_mask = (starts == end_start).astype(jnp.float32)
        joined = (last_start == end_start).astype(jnp.float32)
        kept = key_feats * keep_mask[:, None, None]
        key_state = jnp.einsum('sgf,sgd->gfd', kept, value_block, precision=highest) + joined * key_state
        key_norm = lax.optimization_barrier(jnp.sum(kept, axis=0)) + joined * key_norm
        return ((key_state, key_norm, end_start), outputs)
    step = jax.checkpoint(step)
    initial = (jnp.zeros((key_heads, feat_twice, head_width), jnp.float32), jnp.zeros((key_heads, feat_twice), jnp.float32), jnp.int32(-1))
    _, outputs = lax.scan(step, initial, jnp.arange(block_count, dtype=jnp.int32))
    return outputs.reshape(token_count, head_count, head_width)

def reference(queries, keys, values, feat_q, key_feature_weights, doc_start):
    teacher_out = teacher_attention(queries, keys, values, doc_start)

    def run_student(weight_q, weight_k):
        return student_attention(weight_q, weight_k, queries, keys, values, doc_start)
    student_out, student_pull = jax.vjp(run_student, feat_q, key_feature_weights)
    token_count = queries.shape[0]
    tangent = (student_out - teacher_out.astype(jnp.float32)) / math.sqrt(token_count)
    raw_q, raw_k = student_pull(tangent)
    entry_count = raw_q.size + raw_k.size
    mean_square = (jnp.sum(raw_q * raw_q) + jnp.sum(raw_k * raw_k)) / entry_count
    factor = 1.0 / jnp.sqrt(mean_square + 1e-06)
    return (teacher_out, student_out, raw_q * factor, raw_k * factor)
```

```python
import functools, math
import jax, jax.numpy as jnp
from jax import lax
from jax.experimental import pallas as pl
from jax.experimental.pallas import tpu as pltpu
from jax.sharding import PartitionSpec as P

F32, BF16 = jnp.float32, jnp.bfloat16
NN = (((1,), (0,)), ((), ()))
NT = (((1,), (1,)), ((), ()))
TN = (((0,), (0,)), ((), ()))
LOW = -1e30
SPAN, TILE = 1024, 256


def dot(a, b, dims=NN):
    return lax.dot_general(a, b, dims, preferred_element_type=F32)


def halves(x):
    hi = x.astype(BF16)
    return hi, (x - hi.astype(F32)).astype(BF16)


def dot3(a, b, dims=NN):
    return dot(a[0], b[0], dims) + (dot(a[1], b[0], dims) + dot(a[0], b[1], dims))


def soft(x):
    e = jnp.exp(-jnp.abs(x))
    one = 1.0 + e
    log = jnp.where(e < 1e-3, e * (1.0 - e * (0.5 - e * (1.0 / 3.0))), jnp.log(one))
    return jnp.maximum(x, 0.0) + log, jnp.where(x >= 0.0, 1.0, e) / one


def signed(weight):
    return jnp.concatenate([weight, -weight], axis=1)


def compute(span, tile, tokens, pos, doc_ref, k_ref, v_ref, q_ref, wq_ref, wk_ref,
            t_ref, s_ref, gq_ref, gk_ref,
            top, acc, sig, state, kf_s, bias_s, dstate, dkey, wkt):
    slots = span // 128
    heads = q_ref.shape[0]
    mine, first = pos[0], pos[1]
    begin = mine * 128
    first_slot = first // 128
    blocks = (mine - first_slot + slots - 1) // slots
    logit = math.log2(math.e) / math.sqrt(128)
    lanes = lax.broadcasted_iota(jnp.int32, (1, span), 1)
    ones = jnp.ones((span, 128), BF16)

    def slot_of(i):
        return jnp.minimum(first_slot + i * slots, 64 - slots)

    def loads(i):
        at = slot_of(i)
        k = k_ref[pl.ds(at, slots), 0].reshape(span, 128)
        v = v_ref[pl.ds(at, slots), 0].reshape(span, 128)
        key = at * 128 + lanes
        live = (key >= jnp.maximum(first, (first_slot + i * slots) * 128)) & (key < begin)
        return k, jnp.concatenate([v, ones], axis=1), live

    top[...] = jnp.full_like(top, LOW)
    acc[...] = jnp.zeros_like(acc)
    state[...] = jnp.zeros_like(state)
    dstate[...] = jnp.zeros_like(dstate)
    dkey[...] = jnp.zeros_like(dkey)
    wk2 = halves(signed(wk_ref[0]))
    wk_hl = jnp.concatenate(wk2, axis=0)
    wkt[...] = jnp.concatenate([wk2[0].T, wk2[1].T], axis=1)

    def softmax_step(rows, logits, v2):
        old = top[rows, :]
        new = jnp.maximum(old, jnp.max(logits, axis=1, keepdims=True))
        weight = jnp.exp2(logits - new[:, :1]).astype(BF16)
        shrink = jnp.exp2(old - new)
        top[rows, :] = new
        acc[rows, :] = acc[rows, :] * jnp.concatenate([shrink, shrink], axis=1) + dot(weight, v2)

    def prefix(i, _):
        k, v2, live = loads(i)
        bias = jnp.where(live, 0.0, LOW)
        both = dot(wkt[...], jnp.concatenate([k, k], axis=1), NT)
        feat, slope = soft(both)
        feat = jnp.where(live, feat, 0.0)
        sig[i] = jnp.where(live, slope, 0.0)
        hi, lo = halves(feat)
        state[...] += dot(hi, v2) + dot(lo, v2)

        def rows_of(r, _):
            rows = pl.ds(pl.multiple_of(r * tile, tile), tile)
            q = q_ref[pl.ds(r * (tile // 128), tile // 128)].reshape(tile, 128)
            softmax_step(rows, dot(q, k, NT) * logit + bias, v2)
            return 0

        lax.fori_loop(0, heads * 128 // tile, rows_of, 0, unroll=2)
        return 0

    lax.fori_loop(0, blocks, prefix, 0)

    doc = doc_ref[...]
    at_s = lax.broadcasted_iota(jnp.int32, (128, 128), 1)
    at_t = lax.broadcasted_iota(jnp.int32, (128, 128), 0)
    allowed = (at_s <= at_t) & (at_s + begin >= doc)
    match = (doc == first).astype(F32)
    bias_s[...] = jnp.where(allowed, 0.0, LOW)
    keep = jnp.where(allowed, 1.0, 0.0)
    k = k_ref[mine, 0]
    v = v_ref[mine, 0]
    v2 = jnp.concatenate([v, ones[:128]], axis=1)
    feat, _ = soft(dot(jnp.concatenate([k, k], axis=1), wk_hl))
    kf = halves(feat)
    kf_s[0] = kf[0]
    kf_s[1] = kf[1]
    sh, sl = halves(state[...])
    bh = jnp.concatenate([v2, sh], axis=0)
    bl = jnp.concatenate([jnp.zeros_like(v2), sl], axis=0)
    match2 = jnp.concatenate([match, match], axis=1)

    def head(h, _):
        rows = pl.ds(pl.multiple_of(h * 128, 128), 128)
        q = q_ref[h]
        top[rows, :] = jnp.where(match > 0.0, top[rows, :], LOW)
        acc[rows, :] = acc[rows, :] * match2
        softmax_step(rows, dot(q, k, NT) * logit + bias_s[...], v2)
        total = acc[rows, :]
        teacher = (total[:, :128] / total[:, 128:]).astype(BF16)
        t_ref[h] = teacher
        wq2 = jnp.concatenate(halves(signed(wq_ref[h])), axis=0)
        feat, slope = soft(dot(jnp.concatenate([q, q], axis=1), wq2))
        fh, fl = halves(feat)
        sim = dot3((fh, fl), (kf_s[0], kf_s[1]), NT) * keep
        a = halves(jnp.concatenate([sim, feat * match], axis=1))
        out = dot3(a, (bh, bl))
        inverse = 1.0 / out[:, 128:]
        student = out[:, :128] * inverse
        s_ref[h] = student
        tangent = (student - teacher.astype(F32)) * (inverse * (1.0 / math.sqrt(tokens)))
        loss = -jnp.sum(tangent * student, axis=1, keepdims=True) * (1.0 / 128.0)
        d = jnp.concatenate([tangent, jnp.broadcast_to(loss, (128, 128))], axis=1)
        dh = halves(d)
        da = dot3(dh, (bh, bl), NT)
        dsim = halves(da[:, :128] * keep)
        dfeat = dot3(dsim, (kf_s[0], kf_s[1])) + da[:, 128:] * match
        dp = jnp.concatenate(halves(dfeat * slope), axis=1)
        gt = dot(dp, q, TN)
        gt = gt[:128] + gt[128:]
        gq_ref[h] = gt[:64] - gt[64:]
        dkey[...] += dot3((fh, fl), dsim, TN)
        dm = halves(d * match2)
        dstate[...] += dot3((fh, fl), dm, TN)
        return 0

    lax.fori_loop(0, heads, head, 0)

    both = dot(wkt[...], jnp.concatenate([k, k], axis=1), NT)
    _, slope = soft(both)
    ph, plo = halves(dkey[...] * slope)
    state[:, :128] = dot(ph, k) + dot(plo, k)
    ds = halves(dstate[...])

    def pull(i, _):
        k, v2, _ = loads(i)
        dk = dot(ds[0], v2, NT) + dot(ds[1], v2, NT)
        hi, lo = halves(dk * sig[i])
        state[:, :128] += dot(hi, k) + dot(lo, k)
        return 0

    lax.fori_loop(0, blocks, pull, 0)
    gk_ref[0] = state[:64, :128] - state[64:, :128]


def run(pos, doc, kv, q, wq, wk, tokens, span=512, tile=256):
    groups = wk.shape[0]
    heads = q.shape[0] // groups
    spec = pl.BlockSpec
    return pl.pallas_call(
        functools.partial(compute, span, tile, tokens),
        out_shape=(
            jax.ShapeDtypeStruct(q.shape, BF16),
            jax.ShapeDtypeStruct(q.shape, F32),
            jax.ShapeDtypeStruct((q.shape[0], 64, 128), F32),
            jax.ShapeDtypeStruct((groups, 64, 128), F32),
        ),
        grid=(groups,),
        in_specs=[
            spec(memory_space=pltpu.SMEM),
            spec((128, 128), lambda g: (0, 0)),
            spec((64, 1, 128, 128), lambda g: (0, g, 0, 0)),
            spec((64, 1, 128, 128), lambda g: (0, g + groups, 0, 0)),
            spec((heads, 128, 128), lambda g: (g, 0, 0)),
            spec((heads, 128, 64), lambda g: (g, 0, 0)),
            spec((1, 128, 64), lambda g: (g, 0, 0)),
        ],
        out_specs=(
            spec((heads, 128, 128), lambda g: (g, 0, 0)),
            spec((heads, 128, 128), lambda g: (g, 0, 0)),
            spec((heads, 64, 128), lambda g: (g, 0, 0)),
            spec((1, 64, 128), lambda g: (g, 0, 0)),
        ),
        scratch_shapes=[
            pltpu.VMEM((heads * 128, 128), F32),
            pltpu.VMEM((heads * 128, 256), F32),
            pltpu.VMEM((64 * 128 // span, 128, span), F32),
            pltpu.VMEM((128, 256), F32),
            pltpu.VMEM((2, 128, 128), BF16),
            pltpu.VMEM((128, 128), F32),
            pltpu.VMEM((128, 256), F32),
            pltpu.VMEM((128, 128), F32),
            pltpu.VMEM((128, 256), BF16),
        ],
        compiler_params=pltpu.CompilerParams(dimension_semantics=("arbitrary",), vmem_limit_bytes=58 * 2**20),
    )(pos, doc, kv, kv, q, wq, wk)


MESH = pl.DeviceIdType.MESH


def place():
    at = lax.axis_index("seq")
    return at // 16, (at // 2) % 8, at % 2


def seq_of(y, z, x):
    return {"seq": ((y + 4) % 4 * 8 + (z + 8) % 8) * 2 + x}


def greet(peers):
    barrier = pltpu.get_barrier_semaphore()
    for peer in peers:
        pl.semaphore_signal(barrier, inc=1, device_id=peer, device_id_type=MESH)
    pl.semaphore_wait(barrier, len(peers))


class Copies:
    def __init__(self, out_sem, in_sem):
        self.sems, self.all = (out_sem, in_sem), []

    def __call__(self, src, dst, peer):
        n = len(self.all)
        copy = pltpu.make_async_remote_copy(
            src_ref=src,
            dst_ref=dst,
            send_sem=self.sems[0].at[n],
            recv_sem=self.sems[1].at[n],
            device_id=peer,
            device_id_type=MESH,
        )
        copy.start()
        self.all.append(copy)
        return copy

    def finish(self):
        for copy in self.all:
            copy.wait_send()


PART_A, PART_B, PART_C = (0, 96, 176), (176, 272, 352), (352, 432, 512)


def gather_kernel(own, out, out_sem, in_sem, own_sem):
    y, z, x = place()
    greet(
        [seq_of(y, z, 1 - x)]
        + [seq_of(y + k, z, x) for k in (1, -1)]
        + [seq_of(y, z + k, x) for k in (1, -1)]
    )
    send = Copies(out_sem, in_sem)

    def ring(part, region, axis, source=None):
        size = 8 if axis == "z" else 4
        here = z if axis == "z" else y

        def toward(k):
            return seq_of(y, z + k, x) if axis == "z" else seq_of(y + k, z, x)

        def rows(a, b):
            return pl.ds(part[a], part[b] - part[a])

        for step in range(1, size // 2 + 1):
            last = step == size // 2
            cuts = ((0, 1), (1, 2)) if last else ((0, 2), (0, 2))
            back, fore = (here + size - step + 1) % size, (here + step - 1) % size
            pair = []
            for at, cut, k in ((back, cuts[0], 1), (fore, cuts[1], -1)):
                target = region(at, rows(*cut))
                from_here = source(rows(*cut)) if source is not None and step == 1 else target
                pair.append(send(from_here, target, toward(k)))
            yield
            for copy in pair:
                copy.wait_recv()

    keep = pltpu.make_async_copy(own, out.at[y, z, x], own_sem)
    keep.start()
    rows_c = pl.ds(PART_C[0], PART_C[2] - PART_C[0])
    across = seq_of(y, z, 1 - x)
    first = pl.ds(0, PART_C[0])
    cross = send(own.at[first], out.at[y, z, x, first], across)
    cz = ring(PART_C, lambda i, r: out.at[y, i, x, r], "z", lambda r: own.at[r])
    ay = ring(PART_A, lambda i, r: out.at[i, z, :, r], "y")
    bz = ring(PART_B, lambda i, r: out.at[y, i, :, r], "z")
    az = ring(PART_A, lambda i, r: out.at[:, i, :, r], "z")
    cy = ring(PART_C, lambda i, r: out.at[i, :, x, r], "y")
    by = ring(PART_B, lambda i, r: out.at[i, :, :, r], "y")
    waits = [cross]

    def over(i):
        region = out.at[i, :, x, rows_c]
        waits.append(send(region, region, across))

    def go(stream):
        next(stream, None)

    go(cz)
    keep.wait()
    cross.wait_recv()
    waits.clear()
    go(ay)
    go(bz)
    go(cz)
    go(ay)
    go(bz)
    go(cz)
    go(ay)
    go(az)
    go(bz)
    go(cz)
    go(cz)
    go(cy)
    over(y)
    go(bz)
    go(az)
    go(bz)
    go(by)
    go(cy)
    over((y + 3) % 4)
    over((y + 1) % 4)
    go(az)
    go(cy)
    over((y + 2) % 4)
    go(by)
    go(az)
    go(by)
    go(az)
    for copy in waits:
        copy.wait_recv()
    send.finish()


def gather(own):
    return pl.pallas_call(
        gather_kernel,
        out_shape=jax.ShapeDtypeStruct((4, 8, 2) + own.shape, own.dtype),
        in_specs=[pl.BlockSpec(memory_space=pltpu.VMEM)],
        out_specs=pl.BlockSpec(memory_space=pl.ANY),
        scratch_shapes=[
            pltpu.SemaphoreType.DMA((48,)),
            pltpu.SemaphoreType.DMA((48,)),
            pltpu.SemaphoreType.DMA,
        ],
        compiler_params=pltpu.CompilerParams(collective_id=0, has_side_effects=True),
    )(own)


def reduce_kernel(entries, g, out, far, near, acc, mid, zin, piece, xin, sq, sqin, full, out_sem, in_sem):
    y, z, x = place()
    head = lax.axis_index("head")
    peers_z = [seq_of(y, z + k, x) for k in range(1, 8)]
    peers_h = [{"head": (head + k) % 4} for k in range(1, 4)]
    up, down, across = seq_of(y + 1, z, x), seq_of(y - 1, z, x), seq_of(y, z, 1 - x)
    greet([up, down, across] + peers_z + peers_h)
    send = Copies(out_sem, in_sem)
    lo, hi = pl.ds(0, 4), pl.ds(4, 4)
    opposite, above, below = (y + 2) % 4, (y + 1) % 4, (y + 3) % 4
    far_up = send(g.at[opposite, lo], far.at[0], up)
    far_down = send(g.at[opposite, hi], far.at[1], down)
    near_up = send(g.at[above, hi], near.at[0], up)
    near_down = send(g.at[below, lo], near.at[1], down)
    far_up.wait_recv()
    acc[0] = g[above, lo] + far[0]
    acc_up = send(acc.at[0], near.at[2], up)
    far_down.wait_recv()
    acc[1] = g[below, hi] + far[1]
    acc_down = send(acc.at[1], near.at[3], down)
    near_up.wait_recv()
    near_down.wait_recv()
    acc_up.wait_recv()
    acc_down.wait_recv()
    mid[lo] = g[y, lo] + near[1] + near[2]
    mid[hi] = g[y, hi] + near[0] + near[3]
    parts = [send(mid.at[(z + k) % 8], zin.at[k - 1], peers_z[k - 1]) for k in range(1, 8)]
    total = mid[z]
    for k, part in enumerate(parts):
        part.wait_recv()
        total = total + zin[k]
    piece[...] = total
    swap = send(piece, xin, across)
    swap.wait_recv()
    total = total + xin[...]
    squares = total[0:8] * total[0:8]
    for k in range(1, 9):
        squares = squares + total[8 * k : 8 * k + 8] * total[8 * k : 8 * k + 8]
    sq[...] = squares
    shares = [send(sq, sqin.at[k - 1], peers_h[k - 1]) for k in range(1, 4)]
    full[y, z, 0:72] = total
    for k, share in enumerate(shares):
        share.wait_recv()
        squares = squares + sqin[k]
    full[y, z, 72:80] = squares
    shard = full.at[y, z]
    for part in [send(shard, shard, peer) for peer in peers_z]:
        part.wait_recv()
    slab = full.at[y]
    both = [send(slab, slab, up), send(slab, slab, down)]
    both[0].wait_recv()
    half = full.at[below, lo]
    last = [send(half, half, up)]
    both[1].wait_recv()
    half = full.at[above, hi]
    last.append(send(half, half, down))
    for copy in last:
        copy.wait_recv()
    squares = full[0, 0, 72:80]
    for k in range(1, 32):
        squares = squares + full[k // 8, k % 8, 72:80]
    factor = 1.0 / jnp.sqrt(jnp.broadcast_to(jnp.sum(squares) * (1.0 / entries) + 1e-6, (72, 128)))

    def scale(k, _):
        out[k // 8, k % 8] = full[k // 8, k % 8, 0:72] * factor
        return 0

    lax.fori_loop(0, 32, scale, 0)
    send.finish()


def reduce(g, entries):
    f32 = jnp.float32
    return pl.pallas_call(
        functools.partial(reduce_kernel, entries),
        out_shape=jax.ShapeDtypeStruct((4, 8, 72, 128), f32),
        in_specs=[pl.BlockSpec(memory_space=pltpu.VMEM)],
        out_specs=pl.BlockSpec(memory_space=pltpu.VMEM),
        scratch_shapes=[
            pltpu.VMEM((2, 4, 72, 128), f32),
            pltpu.VMEM((4, 4, 72, 128), f32),
            pltpu.VMEM((2, 4, 72, 128), f32),
            pltpu.VMEM((8, 72, 128), f32),
            pltpu.VMEM((7, 72, 128), f32),
            pltpu.VMEM((72, 128), f32),
            pltpu.VMEM((72, 128), f32),
            pltpu.VMEM((8, 128), f32),
            pltpu.VMEM((3, 8, 128), f32),
            pltpu.VMEM((4, 8, 80, 128), f32),
            pltpu.SemaphoreType.DMA((32,)),
            pltpu.SemaphoreType.DMA((32,)),
        ],
        compiler_params=pltpu.CompilerParams(collective_id=1, has_side_effects=True),
    )(g)


def shards(queries, keys, values, feat_q, key_feature_weights, doc_start):
    rows, heads, width = queries.shape
    groups = keys.shape[1]
    tokens = rows * lax.axis_size("seq")
    kv = jnp.concatenate([keys, values], axis=1).transpose(1, 0, 2).reshape(2 * groups * rows, width)
    gathered = gather(kv).reshape(64, 2 * groups, rows, width)
    q = queries.transpose(1, 0, 2)
    pos = jnp.stack([lax.axis_index("seq").astype(jnp.int32), doc_start[0]])
    doc = jnp.broadcast_to(doc_start[:, None], (rows, rows))
    teacher, student, gq, gk = run(pos, doc, gathered, q, feat_q, key_feature_weights, tokens, SPAN, TILE)
    gk = jnp.pad(gk.reshape(32, 4, 128), ((0, 0), (0, 4), (0, 0)))
    g = jnp.concatenate([gq, gk], axis=1).reshape(4, 8, 72, 128)
    entries = (heads + groups) * lax.axis_size("head") * width * 64
    g = reduce(g, entries).reshape(32, 72, 128)
    gk = g[:, 64:68].reshape(groups, 64, 128)
    return (
        teacher.transpose(1, 0, 2),
        student.transpose(1, 0, 2),
        g[:, :64].transpose(0, 2, 1),
        gk.transpose(0, 2, 1),
    )


def solution(mesh):
    placed = (
        P("seq", "head", None),
        P("seq", "head", None),
        P("seq", "head", None),
        P("head", None, None),
        P("head", None, None),
        P("seq"),
    )
    return jax.shard_map(
        shards,
        mesh=mesh,
        in_specs=placed,
        out_specs=placed[:2] + placed[3:5],
        check_vma=False,
    )
```

```python
import functools, math
import jax, jax.numpy as jnp
from jax import lax
from jax.experimental import pallas as pl
from jax.experimental.pallas import tpu as pltpu
from jax.sharding import PartitionSpec as P

F32, BF16 = jnp.float32, jnp.bfloat16
NN = (((1,), (0,)), ((), ()))
NT = (((1,), (1,)), ((), ()))
TN = (((0,), (0,)), ((), ()))
LOW = -1e30
BATCH = 8
SPAN, TILE = 1024, 128
PASS = (3, 3, 3, 3, 2, 3, 3, 2, 2)


def dot(a, b, dims=NN):
    return lax.dot_general(a, b, dims, preferred_element_type=F32)


def halves(x):
    hi = x.astype(BF16)
    return hi, (x - hi.astype(F32)).astype(BF16)


def soft(x):
    e = jnp.exp(-jnp.abs(x))
    one = 1.0 + e
    log = jnp.where(e < 1e-3, e * (1.0 - e * (0.5 - e * (1.0 / 3.0))), jnp.log(one))
    return e, log, 1.0 / one


def soft_lanes(x):
    e, log, inverse = soft(x)
    return jnp.maximum(x, 0.0) + log, jnp.where(x >= 0.0, 1.0, e) * inverse


def soft_rows(x):
    e, log, inverse = soft(x)
    other = e * inverse
    feat = jnp.concatenate([jnp.maximum(x, 0.0) + log, jnp.maximum(-x, 0.0) + log], axis=0)
    slope = jnp.concatenate(
        [jnp.where(x >= 0.0, inverse, other), jnp.where(x >= 0.0, other, inverse)], axis=0
    )
    return feat, slope


def dots(passes, a, b, dims=NN):
    out = dot(a[0], b[0], dims)
    if passes > 1:
        out = out + dot(a[1], b[0], dims)
    if passes > 2:
        out = out + dot(a[0], b[1], dims)
    return out


def signed(weight):
    return jnp.concatenate([weight, -weight], axis=1)


def compute(span, tile, tokens, pos, doc_ref, k_ref, v_ref, q_ref, wq_ref, wk_ref,
            t_ref, s_ref, gq_ref, gk_ref,
            top, acc, sig, state, dstate, dkey, wkt):
    slots = span // 128
    heads = q_ref.shape[0]
    mine, first = pos[0], pos[1]
    begin = mine * 128
    first_slot = first // 128
    blocks = (mine - first_slot + slots - 1) // slots
    logit = math.log2(math.e) / math.sqrt(128)
    lanes = lax.broadcasted_iota(jnp.int32, (1, span), 1)
    ones = jnp.ones((span, 128), BF16)

    def loads(i):
        at = jnp.minimum(first_slot + i * slots, 64 - slots)
        k = k_ref[pl.ds(at, slots), 0].reshape(span, 128)
        v = v_ref[pl.ds(at, slots), 0].reshape(span, 128)
        key = at * 128 + lanes
        live = (key >= jnp.maximum(first, (first_slot + i * slots) * 128)) & (key < begin)
        return k, jnp.concatenate([v, ones], axis=1), live

    top[...] = jnp.full_like(top, LOW)
    acc[...] = jnp.zeros_like(acc)
    state[...] = jnp.zeros_like(state)
    dstate[...] = jnp.zeros_like(dstate)
    dkey[...] = jnp.zeros_like(dkey)
    wk2 = halves(signed(wk_ref[0]))
    wk_hl = jnp.concatenate(wk2, axis=0)
    wkt[...] = jnp.concatenate([wk2[0].T[:64], wk2[1].T[:64]], axis=1)

    def softmax_step(rows, raw, bias, v2):
        if bias is not None:
            raw = raw + bias
        old = top[rows, :]
        new = jnp.maximum(old, jnp.max(raw, axis=1, keepdims=True))
        base = new * logit
        weight = jnp.exp2(raw * logit - base[:, :1]).astype(BF16)
        shrink = jnp.exp2(old * logit - base)
        top[rows, :] = new
        acc[rows, :] = acc[rows, :] * jnp.concatenate([shrink, shrink], axis=1) + dot(weight, v2)

    def scores(r, k):
        q = q_ref[r * (tile // 128) : (r + 1) * (tile // 128)].reshape(tile, 128)
        return dot(q, k, NT)

    def attend(k, v2, bias):
        count = heads * 128 // tile
        ahead = scores(0, k)
        for r in range(count):
            raw = ahead
            if r + 1 < count:
                ahead = scores(r + 1, k)
            softmax_step(slice(r * tile, (r + 1) * tile), raw, bias, v2)

    def prefix(i, _):
        k, v2, live = loads(i)
        feat, slope = soft_rows(dot(wkt[...], jnp.concatenate([k, k], axis=1), NT))
        feat = jnp.where(live, feat, 0.0)
        sig[i] = jnp.where(live, slope, 0.0)
        hi, lo = halves(feat)
        state[...] += dot(hi, v2) + dot(lo, v2)
        edge = (i == 0) | (i == blocks - 1)

        @pl.when(edge)
        def _():
            attend(k, v2, jnp.where(live, 0.0, LOW))

        @pl.when(jnp.logical_not(edge))
        def _():
            attend(k, v2, None)

        return 0

    lax.fori_loop(0, blocks, prefix, 0)

    doc = doc_ref[...]
    at_s = lax.broadcasted_iota(jnp.int32, (128, 128), 1)
    at_t = lax.broadcasted_iota(jnp.int32, (128, 128), 0)
    allowed = (at_s <= at_t) & (at_s + begin >= doc)

    def spread(x):
        return jnp.concatenate([x] * BATCH, axis=0)

    match = spread((doc == first).astype(F32))
    match2 = jnp.concatenate([match, match], axis=1)
    bias = spread(jnp.where(allowed, 0.0, LOW))
    keep = spread(jnp.where(allowed, 1.0, 0.0))
    k = k_ref[mine, 0]
    v2 = jnp.concatenate([v_ref[mine, 0], ones[:128]], axis=1)
    kf = halves(soft_lanes(dot(jnp.concatenate([k, k], axis=1), wk_hl))[0])
    sh, sl = halves(state[...])
    bh = jnp.concatenate([v2, sh], axis=0)
    bl = jnp.concatenate([jnp.zeros_like(v2), sl], axis=0)
    full = BATCH * 128

    def some(b, _):
        h0 = b * BATCH
        rows = pl.ds(pl.multiple_of(b * full, full), full)
        q = q_ref[pl.ds(h0, BATCH)].reshape(full, 128)
        top[rows, :] = jnp.where(match > 0.0, top[rows, :], LOW)
        acc[rows, :] = acc[rows, :] * match2
        softmax_step(rows, dot(q, k, NT), bias, v2)
        total = acc[rows, :]
        teacher = (total[:, :128] / total[:, 128:]).astype(BF16)
        t_ref[pl.ds(h0, BATCH)] = teacher.reshape(BATCH, 128, 128)
        both = []
        for j in range(BATCH):
            wq2 = jnp.concatenate(halves(signed(wq_ref[h0 + j])), axis=0)
            qj = q_ref[h0 + j]
            both.append(dot(jnp.concatenate([qj, qj], axis=1), wq2))
        feat, slope = soft_lanes(jnp.concatenate(both, axis=0))
        fs = halves(feat)
        sim = dots(PASS[0], fs, kf, NT) * keep
        a = halves(jnp.concatenate([sim, feat * match], axis=1))
        out = dots(PASS[1], a, (bh, bl))
        inverse = 1.0 / out[:, 128:]
        student = out[:, :128] * inverse
        s_ref[pl.ds(h0, BATCH)] = student.reshape(BATCH, 128, 128)
        tangent = (student - teacher.astype(F32)) * (inverse * (1.0 / math.sqrt(tokens)))
        loss = -jnp.sum(tangent * student, axis=1, keepdims=True) * (1.0 / 128.0)
        d = jnp.concatenate([tangent, jnp.broadcast_to(loss, (full, 128))], axis=1)
        da = dots(PASS[2], halves(d), (bh, bl), NT)
        dsim = halves(da[:, :128] * keep)
        dfeat = dots(PASS[3], dsim, kf) + da[:, 128:] * match
        dp = halves(dfeat * slope)
        for j in range(BATCH):
            part = slice(j * 128, (j + 1) * 128)
            gt = dots(PASS[4], (dp[0][part], dp[1][part]), (q_ref[h0 + j],), TN)
            gq_ref[h0 + j] = gt[:64] - gt[64:]
        dkey[...] += dots(PASS[5], fs, dsim, TN)
        dstate[...] += dots(PASS[6], fs, halves(d * match2), TN)
        return 0

    lax.fori_loop(0, heads // BATCH, some, 0)

    _, slope = soft_rows(dot(wkt[...], jnp.concatenate([k, k], axis=1), NT))
    ph, plo = halves(dkey[...] * slope)
    state[:, :128] = dot(ph, k) + dot(plo, k)
    ds = halves(dstate[...])

    def pull(i, _):
        k, v2, _ = loads(i)
        dk = dots(PASS[7], ds, (v2,), NT)
        state[:, :128] += dots(PASS[8], halves(dk * sig[i]), (k,))
        return 0

    lax.fori_loop(0, blocks, pull, 0)
    gk_ref[0] = state[:64, :128] - state[64:, :128]


def run(pos, doc, kv, q, wq, wk, tokens, span=512, tile=256):
    groups = wk.shape[0]
    heads = q.shape[0] // groups
    spec = pl.BlockSpec
    return pl.pallas_call(
        functools.partial(compute, span, tile, tokens),
        out_shape=(
            jax.ShapeDtypeStruct(q.shape, BF16),
            jax.ShapeDtypeStruct(q.shape, F32),
            jax.ShapeDtypeStruct((q.shape[0], 64, 128), F32),
            jax.ShapeDtypeStruct((groups, 64, 128), F32),
        ),
        grid=(groups,),
        in_specs=[
            spec(memory_space=pltpu.SMEM),
            spec((128, 128), lambda g: (0, 0)),
            spec((64, 1, 128, 128), lambda g: (0, g, 0, 0)),
            spec((64, 1, 128, 128), lambda g: (0, g + groups, 0, 0)),
            spec((heads, 128, 128), lambda g: (g, 0, 0)),
            spec((heads, 128, 64), lambda g: (g, 0, 0)),
            spec((1, 128, 64), lambda g: (g, 0, 0)),
        ],
        out_specs=(
            spec((heads, 128, 128), lambda g: (g, 0, 0)),
            spec((heads, 128, 128), lambda g: (g, 0, 0)),
            spec((heads, 64, 128), lambda g: (g, 0, 0)),
            spec((1, 64, 128), lambda g: (g, 0, 0)),
        ),
        scratch_shapes=[
            pltpu.VMEM((heads * 128, 128), F32),
            pltpu.VMEM((heads * 128, 256), F32),
            pltpu.VMEM((64 * 128 // span, 128, span), F32),
            pltpu.VMEM((128, 256), F32),
            pltpu.VMEM((128, 256), F32),
            pltpu.VMEM((128, 128), F32),
            pltpu.VMEM((64, 256), BF16),
        ],
        compiler_params=pltpu.CompilerParams(dimension_semantics=("arbitrary",), vmem_limit_bytes=58 * 2**20),
    )(pos, doc, kv, kv, q, wq, wk)


MESH = pl.DeviceIdType.MESH


def place():
    at = lax.axis_index("seq")
    return at // 16, (at // 2) % 8, at % 2


def seq_of(y, z, x):
    return {"seq": ((y + 4) % 4 * 8 + (z + 8) % 8) * 2 + x}


def greet(peers):
    barrier = pltpu.get_barrier_semaphore()
    for peer in peers:
        pl.semaphore_signal(barrier, inc=1, device_id=peer, device_id_type=MESH)
    pl.semaphore_wait(barrier, len(peers))


class Copies:
    def __init__(self, out_sem, in_sem):
        self.sems, self.all = (out_sem, in_sem), []

    def __call__(self, src, dst, peer):
        n = len(self.all)
        copy = pltpu.make_async_remote_copy(
            src_ref=src,
            dst_ref=dst,
            send_sem=self.sems[0].at[n],
            recv_sem=self.sems[1].at[n],
            device_id=peer,
            device_id_type=MESH,
        )
        copy.start()
        self.all.append(copy)
        return copy

    def finish(self):
        for copy in self.all:
            copy.wait_send()


PART_A, PART_B, PART_C = (0, 96, 176), (176, 272, 352), (352, 432, 512)


def gather_kernel(own, out, out_sem, in_sem, own_sem):
    y, z, x = place()
    greet(
        [seq_of(y, z, 1 - x)]
        + [seq_of(y + k, z, x) for k in (1, -1)]
        + [seq_of(y, z + k, x) for k in (1, -1)]
    )
    send = Copies(out_sem, in_sem)

    def ring(part, region, axis, source=None):
        size = 8 if axis == "z" else 4
        here = z if axis == "z" else y

        def toward(k):
            return seq_of(y, z + k, x) if axis == "z" else seq_of(y + k, z, x)

        def rows(a, b):
            return pl.ds(part[a], part[b] - part[a])

        for step in range(1, size // 2 + 1):
            last = step == size // 2
            cuts = ((0, 1), (1, 2)) if last else ((0, 2), (0, 2))
            back, fore = (here + size - step + 1) % size, (here + step - 1) % size
            pair = []
            for at, cut, k in ((back, cuts[0], 1), (fore, cuts[1], -1)):
                target = region(at, rows(*cut))
                from_here = source(rows(*cut)) if source is not None and step == 1 else target
                pair.append(send(from_here, target, toward(k)))
            yield
            for copy in pair:
                copy.wait_recv()

    keep = pltpu.make_async_copy(own, out.at[y, z, x], own_sem)
    keep.start()
    rows_c = pl.ds(PART_C[0], PART_C[2] - PART_C[0])
    across = seq_of(y, z, 1 - x)
    first = pl.ds(0, PART_C[0])
    cross = send(own.at[first], out.at[y, z, x, first], across)
    cz = ring(PART_C, lambda i, r: out.at[y, i, x, r], "z", lambda r: own.at[r])
    ay = ring(PART_A, lambda i, r: out.at[i, z, :, r], "y")
    bz = ring(PART_B, lambda i, r: out.at[y, i, :, r], "z")
    az = ring(PART_A, lambda i, r: out.at[:, i, :, r], "z")
    cy = ring(PART_C, lambda i, r: out.at[i, :, x, r], "y")
    by = ring(PART_B, lambda i, r: out.at[i, :, :, r], "y")
    waits = [cross]

    def over(i):
        region = out.at[i, :, x, rows_c]
        waits.append(send(region, region, across))

    def go(stream):
        next(stream, None)

    go(cz)
    keep.wait()
    cross.wait_recv()
    waits.clear()
    go(ay)
    go(bz)
    go(cz)
    go(ay)
    go(bz)
    go(cz)
    go(ay)
    go(az)
    go(bz)
    go(cz)
    go(cz)
    go(cy)
    over(y)
    go(bz)
    go(az)
    go(bz)
    go(by)
    go(cy)
    over((y + 3) % 4)
    over((y + 1) % 4)
    go(az)
    go(cy)
    over((y + 2) % 4)
    go(by)
    go(az)
    go(by)
    go(az)
    for copy in waits:
        copy.wait_recv()
    send.finish()


def gather(own):
    return pl.pallas_call(
        gather_kernel,
        out_shape=jax.ShapeDtypeStruct((4, 8, 2) + own.shape, own.dtype),
        in_specs=[pl.BlockSpec(memory_space=pltpu.VMEM)],
        out_specs=pl.BlockSpec(memory_space=pl.ANY),
        scratch_shapes=[
            pltpu.SemaphoreType.DMA((48,)),
            pltpu.SemaphoreType.DMA((48,)),
            pltpu.SemaphoreType.DMA,
        ],
        compiler_params=pltpu.CompilerParams(collective_id=0, has_side_effects=True),
    )(own)


def reduce_kernel(entries, g, out, far, near, acc, mid, zin, piece, xin, sq, sqin, full, out_sem, in_sem):
    y, z, x = place()
    head = lax.axis_index("head")
    peers_z = [seq_of(y, z + k, x) for k in range(1, 8)]
    peers_h = [{"head": (head + k) % 4} for k in range(1, 4)]
    up, down, across = seq_of(y + 1, z, x), seq_of(y - 1, z, x), seq_of(y, z, 1 - x)
    greet([up, down, across] + peers_z + peers_h)
    send = Copies(out_sem, in_sem)
    lo, hi = pl.ds(0, 4), pl.ds(4, 4)
    opposite, above, below = (y + 2) % 4, (y + 1) % 4, (y + 3) % 4
    far_up = send(g.at[opposite, lo], far.at[0], up)
    far_down = send(g.at[opposite, hi], far.at[1], down)
    near_up = send(g.at[above, hi], near.at[0], up)
    near_down = send(g.at[below, lo], near.at[1], down)
    far_up.wait_recv()
    acc[0] = g[above, lo] + far[0]
    acc_up = send(acc.at[0], near.at[2], up)
    far_down.wait_recv()
    acc[1] = g[below, hi] + far[1]
    acc_down = send(acc.at[1], near.at[3], down)
    near_up.wait_recv()
    near_down.wait_recv()
    acc_up.wait_recv()
    acc_down.wait_recv()
    mid[lo] = g[y, lo] + near[1] + near[2]
    mid[hi] = g[y, hi] + near[0] + near[3]
    parts = [send(mid.at[(z + k) % 8], zin.at[k - 1], peers_z[k - 1]) for k in range(1, 8)]
    total = mid[z]
    for k, part in enumerate(parts):
        part.wait_recv()
        total = total + zin[k]
    piece[...] = total
    swap = send(piece, xin, across)
    swap.wait_recv()
    total = total + xin[...]
    squares = total[0:8] * total[0:8]
    for k in range(1, 9):
        squares = squares + total[8 * k : 8 * k + 8] * total[8 * k : 8 * k + 8]
    sq[...] = squares
    shares = [send(sq, sqin.at[k - 1], peers_h[k - 1]) for k in range(1, 4)]
    full[y, z, 0:72] = total
    for k, share in enumerate(shares):
        share.wait_recv()
        squares = squares + sqin[k]
    full[y, z, 72:80] = squares
    shard = full.at[y, z]
    for part in [send(shard, shard, peer) for peer in peers_z]:
        part.wait_recv()
    slab = full.at[y]
    both = [send(slab, slab, up), send(slab, slab, down)]
    both[0].wait_recv()
    half = full.at[below, lo]
    last = [send(half, half, up)]
    both[1].wait_recv()
    half = full.at[above, hi]
    last.append(send(half, half, down))
    for copy in last:
        copy.wait_recv()
    squares = full[0, 0, 72:80]
    for k in range(1, 32):
        squares = squares + full[k // 8, k % 8, 72:80]
    factor = 1.0 / jnp.sqrt(jnp.broadcast_to(jnp.sum(squares) * (1.0 / entries) + 1e-6, (72, 128)))

    def scale(k, _):
        out[k // 8, k % 8] = full[k // 8, k % 8, 0:72] * factor
        return 0

    lax.fori_loop(0, 32, scale, 0)
    send.finish()


def reduce(g, entries):
    f32 = jnp.float32
    return pl.pallas_call(
        functools.partial(reduce_kernel, entries),
        out_shape=jax.ShapeDtypeStruct((4, 8, 72, 128), f32),
        in_specs=[pl.BlockSpec(memory_space=pltpu.VMEM)],
        out_specs=pl.BlockSpec(memory_space=pltpu.VMEM),
        scratch_shapes=[
            pltpu.VMEM((2, 4, 72, 128), f32),
            pltpu.VMEM((4, 4, 72, 128), f32),
            pltpu.VMEM((2, 4, 72, 128), f32),
            pltpu.VMEM((8, 72, 128), f32),
            pltpu.VMEM((7, 72, 128), f32),
            pltpu.VMEM((72, 128), f32),
            pltpu.VMEM((72, 128), f32),
            pltpu.VMEM((8, 128), f32),
            pltpu.VMEM((3, 8, 128), f32),
            pltpu.VMEM((4, 8, 80, 128), f32),
            pltpu.SemaphoreType.DMA((32,)),
            pltpu.SemaphoreType.DMA((32,)),
        ],
        compiler_params=pltpu.CompilerParams(collective_id=1, has_side_effects=True),
    )(g)


def shards(queries, keys, values, feat_q, key_feature_weights, doc_start):
    rows, heads, width = queries.shape
    groups = keys.shape[1]
    tokens = rows * lax.axis_size("seq")
    kv = jnp.concatenate([keys, values], axis=1).transpose(1, 0, 2).reshape(2 * groups * rows, width)
    gathered = gather(kv).reshape(64, 2 * groups, rows, width)
    q = queries.transpose(1, 0, 2)
    pos = jnp.stack([lax.axis_index("seq").astype(jnp.int32), doc_start[0]])
    doc = jnp.broadcast_to(doc_start[:, None], (rows, rows))
    teacher, student, gq, gk = run(pos, doc, gathered, q, feat_q, key_feature_weights, tokens, SPAN, TILE)
    gk = jnp.pad(gk.reshape(32, 4, 128), ((0, 0), (0, 4), (0, 0)))
    g = jnp.concatenate([gq, gk], axis=1).reshape(4, 8, 72, 128)
    entries = (heads + groups) * lax.axis_size("head") * width * 64
    g = reduce(g, entries).reshape(32, 72, 128)
    gk = g[:, 64:68].reshape(groups, 64, 128)
    return (
        teacher.transpose(1, 0, 2),
        student.transpose(1, 0, 2),
        g[:, :64].transpose(0, 2, 1),
        gk.transpose(0, 2, 1),
    )


def solution(mesh):
    placed = (
        P("seq", "head", None),
        P("seq", "head", None),
        P("seq", "head", None),
        P("head", None, None),
        P("head", None, None),
        P("seq"),
    )
    return jax.shard_map(
        shards,
        mesh=mesh,
        in_specs=placed,
        out_specs=placed[:2] + placed[3:5],
        check_vma=False,
    )
```

```python
import functools, math
import jax, jax.numpy as jnp
from jax import lax
from jax.experimental import pallas as pl
from jax.experimental.pallas import tpu as pltpu
from jax.sharding import PartitionSpec as P

F32, BF16 = jnp.float32, jnp.bfloat16
NN = (((1,), (0,)), ((), ()))
NT = (((1,), (1,)), ((), ()))
TN = (((0,), (0,)), ((), ()))
LOW = -1e30
BATCH = 8
SPAN, TILE = 1024, 128
PASS = (3, 3, 3, 3, 2, 3, 3, 2, 2)


def dot(a, b, dims=NN):
    return lax.dot_general(a, b, dims, preferred_element_type=F32)


def halves(x):
    hi = x.astype(BF16)
    return hi, (x - hi.astype(F32)).astype(BF16)


def soft(x):
    e = jnp.exp(-jnp.abs(x))
    one = 1.0 + e
    log = jnp.where(e < 1e-3, e * (1.0 - e * (0.5 - e * (1.0 / 3.0))), jnp.log(one))
    return e, log, 1.0 / one


def soft_lanes(x):
    e, log, inverse = soft(x)
    return jnp.maximum(x, 0.0) + log, jnp.where(x >= 0.0, 1.0, e) * inverse


def soft_rows(x):
    e, log, inverse = soft(x)
    other = e * inverse
    feat = jnp.concatenate([jnp.maximum(x, 0.0) + log, jnp.maximum(-x, 0.0) + log], axis=0)
    slope = jnp.concatenate(
        [jnp.where(x >= 0.0, inverse, other), jnp.where(x >= 0.0, other, inverse)], axis=0
    )
    return feat, slope


def stacked(a, b):
    both = dot(jnp.concatenate(a, axis=0), b)
    return both[: both.shape[0] // 2] + both[both.shape[0] // 2 :]


def dots(passes, a, b, dims=NN):
    out = dot(a[0], b[0], dims)
    if passes > 1:
        out = out + dot(a[1], b[0], dims)
    if passes > 2:
        out = out + dot(a[0], b[1], dims)
    return out


def signed(weight):
    return jnp.concatenate([weight, -weight], axis=0)


def compute(span, tile, tokens, pos, doc_ref, k_ref, v_ref, q_ref, wq_ref, wk_ref,
            t_ref, s_ref, g_ref,
            top, acc, sig, state, dstate, dkey, wide, q_s):
    slots = span // 128
    heads = q_ref.shape[1]
    mine, first = lax.axis_index("seq"), pos[0]
    begin = mine * 128
    first_slot = first // 128
    blocks = (mine - first_slot + slots - 1) // slots
    logit = math.log2(math.e) / math.sqrt(128)
    lanes = lax.broadcasted_iota(jnp.int32, (1, span), 1)
    ones = jnp.ones((span, 128), BF16)

    def loads(i):
        at = jnp.minimum(first_slot + i * slots, 64 - slots)
        k = k_ref[pl.ds(at, slots), 0].reshape(span, 128)
        v = v_ref[pl.ds(at, slots), 0].reshape(span, 128)
        key = at * 128 + lanes
        live = (key >= jnp.maximum(first, (first_slot + i * slots) * 128)) & (key < begin)
        return k, jnp.concatenate([v, ones], axis=1), live

    top[...] = jnp.full_like(top, LOW)
    acc[...] = jnp.zeros_like(acc)
    state[...] = jnp.zeros_like(state)
    dstate[...] = jnp.zeros_like(dstate)
    dkey[...] = jnp.zeros_like(dkey)
    wkt = jnp.concatenate(halves(wk_ref[0]), axis=1)
    wide[...] = q_ref[...].astype(F32)
    for h in range(heads):
        q_s[h] = wide[:, h, :].astype(BF16)

    def softmax_step(rows, raw, bias, v2):
        if bias is not None:
            raw = raw + bias
        old = top[rows, :]
        new = jnp.maximum(old, jnp.max(raw, axis=1, keepdims=True))
        base = new * logit
        weight = jnp.exp2(raw * logit - base[:, :1]).astype(BF16)
        shrink = jnp.exp2(old * logit - base)
        top[rows, :] = new
        acc[rows, :] = acc[rows, :] * jnp.concatenate([shrink, shrink], axis=1) + dot(weight, v2)

    def scores(r, k):
        q = q_s[r * (tile // 128) : (r + 1) * (tile // 128)].reshape(tile, 128)
        return dot(q, k, NT)

    def attend(k, v2, bias):
        count = heads * 128 // tile
        ahead = scores(0, k)
        for r in range(count):
            raw = ahead
            if r + 1 < count:
                ahead = scores(r + 1, k)
            softmax_step(slice(r * tile, (r + 1) * tile), raw, bias, v2)

    def prefix(i, _):
        k, v2, live = loads(i)
        feat, slope = soft_rows(dot(wkt, jnp.concatenate([k, k], axis=1), NT))
        feat = jnp.where(live, feat, 0.0)
        sig[i] = jnp.where(live, slope, 0.0)
        state[...] += stacked(halves(feat), v2)
        edge = (i == 0) | (i == blocks - 1)

        @pl.when(edge)
        def _():
            attend(k, v2, jnp.where(live, 0.0, LOW))

        @pl.when(jnp.logical_not(edge))
        def _():
            attend(k, v2, None)

        return 0

    lax.fori_loop(0, blocks, prefix, 0)

    doc = jnp.broadcast_to(doc_ref[...], (128, 128)).T
    at_s = lax.broadcasted_iota(jnp.int32, (128, 128), 1)
    at_t = lax.broadcasted_iota(jnp.int32, (128, 128), 0)
    allowed = (at_s <= at_t) & (at_s + begin >= doc)

    def spread(x):
        return jnp.concatenate([x] * BATCH, axis=0)

    match = spread((doc == first).astype(F32))
    match2 = jnp.concatenate([match, match], axis=1)
    bias = spread(jnp.where(allowed, 0.0, LOW))
    keep = spread(jnp.where(allowed, 1.0, 0.0))
    k = k_ref[mine, 0]
    v2 = jnp.concatenate([v_ref[mine, 0], ones[:128]], axis=1)
    kk = jnp.concatenate([k, k], axis=1)
    kf = halves(soft_lanes(dot(kk, signed(wkt), NT))[0])
    sh, sl = halves(state[...])
    bh = jnp.concatenate([v2, sh], axis=0)
    bl = jnp.concatenate([jnp.zeros_like(v2), sl], axis=0)
    full = BATCH * 128

    def some(b, _):
        h0 = b * BATCH
        rows = pl.ds(pl.multiple_of(b * full, full), full)
        q = q_s[pl.ds(h0, BATCH)].reshape(full, 128)
        top[rows, :] = jnp.where(match > 0.0, top[rows, :], LOW)
        acc[rows, :] = acc[rows, :] * match2
        softmax_step(rows, dot(q, k, NT), bias, v2)
        total = acc[rows, :]
        teacher = (total[:, :128] / total[:, 128:]).astype(BF16)
        for j in range(BATCH):
            wide[:, h0 + j, :] = teacher[j * 128 : (j + 1) * 128].astype(F32)
        both = []
        for j in range(BATCH):
            wq2 = signed(jnp.concatenate(halves(wq_ref[h0 + j]), axis=1))
            qj = q_s[h0 + j]
            both.append(dot(jnp.concatenate([qj, qj], axis=1), wq2, NT))
        feat, slope = soft_lanes(jnp.concatenate(both, axis=0))
        fs = halves(feat)
        sim = dots(PASS[0], fs, kf, NT) * keep
        a = halves(jnp.concatenate([sim, feat * match], axis=1))
        out = dots(PASS[1], a, (bh, bl))
        inverse = 1.0 / out[:, 128:]
        student = out[:, :128] * inverse
        for j in range(BATCH):
            s_ref[:, h0 + j, :] = student[j * 128 : (j + 1) * 128]
        tangent = (student - teacher.astype(F32)) * (inverse * (1.0 / math.sqrt(tokens)))
        loss = -jnp.sum(tangent * student, axis=1, keepdims=True) * (1.0 / 128.0)
        d = jnp.concatenate([tangent, jnp.broadcast_to(loss, (full, 128))], axis=1)
        da = dots(PASS[2], halves(d), (bh, bl), NT)
        dsim = halves(da[:, :128] * keep)
        dfeat = dots(PASS[3], dsim, kf) + da[:, 128:] * match
        dp = halves(dfeat * slope)
        for j in range(BATCH):
            part = slice(j * 128, (j + 1) * 128)
            gt = dots(PASS[4], (dp[0][part], dp[1][part]), (q_s[h0 + j],), TN)
            g_ref[h0 + j, 0:64] = gt[:64] - gt[64:]
        dkey[...] += dots(PASS[5], fs, dsim, TN)
        dstate[...] += dots(PASS[6], fs, halves(d * match2), TN)
        return 0

    for b in range(heads // BATCH):
        some(b, 0)
    t_ref[...] = wide[...].astype(BF16)

    _, slope = soft_rows(dot(wkt, kk, NT))
    state[:, :128] = stacked(halves(dkey[...] * slope), k)
    ds = jnp.concatenate(halves(dstate[...]), axis=0)

    def pull(i, _):
        k, v2, _ = loads(i)
        dk = dot(ds, v2, NT)
        state[:, :128] += stacked(halves((dk[:128] + dk[128:]) * sig[i]), k)
        return 0

    lax.fori_loop(0, blocks, pull, 0)
    gk = state[:64, :128] - state[64:, :128]
    pad = jnp.zeros((4, 128), F32)
    for j in range(heads):
        g_ref[j, 64:72] = jnp.concatenate([gk[4 * j : 4 * j + 4], pad], axis=0)


def run(doc, kv, q, wq, wk, tokens, span, tile):
    groups = wk.shape[0]
    heads = q.shape[1] // groups
    spec = pl.BlockSpec
    return pl.pallas_call(
        functools.partial(compute, span, tile, tokens),
        out_shape=(
            jax.ShapeDtypeStruct(q.shape, BF16),
            jax.ShapeDtypeStruct(q.shape, F32),
            jax.ShapeDtypeStruct((q.shape[1], 72, 128), F32),
        ),
        grid=(groups,),
        in_specs=[
            spec(memory_space=pltpu.SMEM),
            spec((1, 128), lambda g: (0, 0)),
            spec((64, 1, 128, 128), lambda g: (0, g, 0, 0)),
            spec((64, 1, 128, 128), lambda g: (0, g + groups, 0, 0)),
            spec((128, heads, 128), lambda g: (0, g, 0)),
            spec((heads, 64, 128), lambda g: (g, 0, 0)),
            spec((1, 64, 128), lambda g: (g, 0, 0)),
        ],
        out_specs=(
            spec((128, heads, 128), lambda g: (0, g, 0)),
            spec((128, heads, 128), lambda g: (0, g, 0)),
            spec((heads, 72, 128), lambda g: (g, 0, 0)),
        ),
        scratch_shapes=[
            pltpu.VMEM((heads * 128, 128), F32),
            pltpu.VMEM((heads * 128, 256), F32),
            pltpu.VMEM((64 * 128 // span, 128, span), F32),
            pltpu.VMEM((128, 256), F32),
            pltpu.VMEM((128, 256), F32),
            pltpu.VMEM((128, 128), F32),
            pltpu.VMEM((128, heads, 128), F32),
            pltpu.VMEM((heads, 128, 128), BF16),
        ],
        compiler_params=pltpu.CompilerParams(
            dimension_semantics=("arbitrary",), vmem_limit_bytes=58 * 2**20
        ),
    )(doc, doc.reshape(1, 128), kv, kv, q, wq, wk)


MESH = pl.DeviceIdType.MESH


def place():
    at = lax.axis_index("seq")
    return at // 16, (at // 2) % 8, at % 2


def seq_of(y, z, x):
    return {"seq": ((y + 4) % 4 * 8 + (z + 8) % 8) * 2 + x}


def greet(peers):
    barrier = pltpu.get_barrier_semaphore()
    for peer in peers:
        pl.semaphore_signal(barrier, inc=1, device_id=peer, device_id_type=MESH)
    pl.semaphore_wait(barrier, len(peers))


class Copies:
    def __init__(self, out_sem, in_sem):
        self.sems, self.all = (out_sem, in_sem), []

    def __call__(self, src, dst, peer):
        n = len(self.all)
        copy = pltpu.make_async_remote_copy(
            src_ref=src,
            dst_ref=dst,
            send_sem=self.sems[0].at[n],
            recv_sem=self.sems[1].at[n],
            device_id=peer,
            device_id_type=MESH,
        )
        copy.start()
        self.all.append(copy)
        return copy

    def finish(self):
        for copy in self.all:
            copy.wait_send()


PART_A, PART_B, PART_C = (0, 96, 176), (176, 272, 352), (352, 432, 512)


def gather_kernel(own, out, out_sem, in_sem, own_sem):
    y, z, x = place()
    greet(
        [seq_of(y, z, 1 - x)]
        + [seq_of(y + k, z, x) for k in (1, -1)]
        + [seq_of(y, z + k, x) for k in (1, -1)]
    )
    send = Copies(out_sem, in_sem)

    def ring(part, region, axis, source=None):
        size = 8 if axis == "z" else 4
        here = z if axis == "z" else y

        def toward(k):
            return seq_of(y, z + k, x) if axis == "z" else seq_of(y + k, z, x)

        def rows(a, b):
            return pl.ds(part[a], part[b] - part[a])

        for step in range(1, size // 2 + 1):
            last = step == size // 2
            cuts = ((0, 1), (1, 2)) if last else ((0, 2), (0, 2))
            back, fore = (here + size - step + 1) % size, (here + step - 1) % size
            pair = []
            for at, cut, k in ((back, cuts[0], 1), (fore, cuts[1], -1)):
                target = region(at, rows(*cut))
                from_here = source(rows(*cut)) if source is not None and step == 1 else target
                pair.append(send(from_here, target, toward(k)))
            yield
            for copy in pair:
                copy.wait_recv()

    keep = pltpu.make_async_copy(own, out.at[y, z, x], own_sem)
    keep.start()
    rows_c = pl.ds(PART_C[0], PART_C[2] - PART_C[0])
    across = seq_of(y, z, 1 - x)
    first = pl.ds(0, PART_C[0])
    cross = send(own.at[first], out.at[y, z, x, first], across)
    cz = ring(PART_C, lambda i, r: out.at[y, i, x, r], "z", lambda r: own.at[r])
    ay = ring(PART_A, lambda i, r: out.at[i, z, :, r], "y")
    bz = ring(PART_B, lambda i, r: out.at[y, i, :, r], "z")
    az = ring(PART_A, lambda i, r: out.at[:, i, :, r], "z")
    cy = ring(PART_C, lambda i, r: out.at[i, :, x, r], "y")
    by = ring(PART_B, lambda i, r: out.at[i, :, :, r], "y")
    waits = [cross]

    def over(i):
        region = out.at[i, :, x, rows_c]
        waits.append(send(region, region, across))

    def go(stream):
        next(stream, None)

    go(cz)
    keep.wait()
    cross.wait_recv()
    waits.clear()
    go(ay)
    go(bz)
    go(cz)
    go(ay)
    go(bz)
    go(cz)
    go(ay)
    go(az)
    go(bz)
    go(cz)
    go(cz)
    go(cy)
    over(y)
    go(bz)
    go(az)
    go(bz)
    go(by)
    go(cy)
    over((y + 3) % 4)
    over((y + 1) % 4)
    go(az)
    go(cy)
    over((y + 2) % 4)
    go(by)
    go(az)
    go(by)
    go(az)
    for copy in waits:
        copy.wait_recv()
    send.finish()


def gather(own):
    return pl.pallas_call(
        gather_kernel,
        out_shape=jax.ShapeDtypeStruct((4, 8, 2) + own.shape, own.dtype),
        in_specs=[pl.BlockSpec(memory_space=pltpu.VMEM)],
        out_specs=pl.BlockSpec(memory_space=pl.ANY),
        scratch_shapes=[
            pltpu.SemaphoreType.DMA((48,)),
            pltpu.SemaphoreType.DMA((48,)),
            pltpu.SemaphoreType.DMA,
        ],
        compiler_params=pltpu.CompilerParams(collective_id=0, has_side_effects=True),
    )(own)


def reduce_kernel(entries, g, out_q, out_k, far, near, acc, mid, zin, piece, xin, sq, sqin, full, out_sem, in_sem):
    y, z, x = place()
    head = lax.axis_index("head")
    peers_z = [seq_of(y, z + k, x) for k in range(1, 8)]
    peers_h = [{"head": (head + k) % 4} for k in range(1, 4)]
    up, down, across = seq_of(y + 1, z, x), seq_of(y - 1, z, x), seq_of(y, z, 1 - x)
    greet([up, down, across] + peers_z + peers_h)
    send = Copies(out_sem, in_sem)
    lo, hi = pl.ds(0, 4), pl.ds(4, 4)
    opposite, above, below = (y + 2) % 4, (y + 1) % 4, (y + 3) % 4
    far_up = send(g.at[opposite, lo], far.at[0], up)
    far_down = send(g.at[opposite, hi], far.at[1], down)
    near_up = send(g.at[above, hi], near.at[0], up)
    near_down = send(g.at[below, lo], near.at[1], down)
    far_up.wait_recv()
    acc[0] = g[above, lo] + far[0]
    acc_up = send(acc.at[0], near.at[2], up)
    far_down.wait_recv()
    acc[1] = g[below, hi] + far[1]
    acc_down = send(acc.at[1], near.at[3], down)
    near_up.wait_recv()
    near_down.wait_recv()
    acc_up.wait_recv()
    acc_down.wait_recv()
    mid[lo] = g[y, lo] + near[1] + near[2]
    mid[hi] = g[y, hi] + near[0] + near[3]
    parts = [send(mid.at[(z + k) % 8], zin.at[k - 1], peers_z[k - 1]) for k in range(1, 8)]
    total = mid[z]
    for k, part in enumerate(parts):
        part.wait_recv()
        total = total + zin[k]
    piece[...] = total
    swap = send(piece, xin, across)
    swap.wait_recv()
    total = total + xin[...]
    squares = total[0:8] * total[0:8]
    for k in range(1, 9):
        squares = squares + total[8 * k : 8 * k + 8] * total[8 * k : 8 * k + 8]
    sq[...] = squares
    shares = [send(sq, sqin.at[k - 1], peers_h[k - 1]) for k in range(1, 4)]
    full[y, z, 0:64] = total[0:64].astype(jnp.bfloat16)
    for k, share in enumerate(shares):
        share.wait_recv()
        squares = squares + sqin[k]
    squares = jnp.sum(squares, axis=0, keepdims=True)
    coarse = squares.astype(jnp.bfloat16).astype(jnp.float32)
    row = lax.broadcasted_iota(jnp.int32, (8, 128), 0)
    pair = jnp.where(row == 0, coarse, jnp.where(row == 1, squares - coarse, 0.0))
    full[y, z, 64:80] = jnp.concatenate([total[64:72], pair], axis=0).astype(jnp.bfloat16)
    shard = full.at[y, z]
    for part in [send(shard, shard, peer) for peer in peers_z]:
        part.wait_recv()
    slab = full.at[y]
    both = [send(slab, slab, up), send(slab, slab, down)]
    both[0].wait_recv()
    half = full.at[below, lo]
    last = [send(half, half, up)]
    both[1].wait_recv()
    half = full.at[above, hi]
    last.append(send(half, half, down))
    for copy in last:
        copy.wait_recv()
    ends = [full[k // 8, k % 8, 64:80].astype(jnp.float32) for k in range(32)]
    squares = ends[0][8:16]
    for end in ends[1:]:
        squares = squares + end[8:16]
    factor = 1.0 / jnp.sqrt(jnp.broadcast_to(jnp.sum(squares) * (1.0 / entries) + 1e-6, (64, 128)))
    for k, end in enumerate(ends):
        out_k[k // 16, 4 * (k % 16) : 4 * (k % 16) + 4] = end[0:4] * factor[0:4]

    def scale(k, _):
        out_q[k] = full[k // 8, k % 8, 0:64].astype(jnp.float32) * factor
        return 0

    lax.fori_loop(0, 32, scale, 0)
    send.finish()


def reduce(g, entries):
    f32 = jnp.float32
    return pl.pallas_call(
        functools.partial(reduce_kernel, entries),
        out_shape=(
            jax.ShapeDtypeStruct((32, 64, 128), f32),
            jax.ShapeDtypeStruct((2, 64, 128), f32),
        ),
        in_specs=[pl.BlockSpec(memory_space=pltpu.VMEM)],
        out_specs=(pl.BlockSpec(memory_space=pltpu.VMEM),) * 2,
        scratch_shapes=[
            pltpu.VMEM((2, 4, 72, 128), f32),
            pltpu.VMEM((4, 4, 72, 128), f32),
            pltpu.VMEM((2, 4, 72, 128), f32),
            pltpu.VMEM((8, 72, 128), f32),
            pltpu.VMEM((7, 72, 128), f32),
            pltpu.VMEM((72, 128), f32),
            pltpu.VMEM((72, 128), f32),
            pltpu.VMEM((8, 128), f32),
            pltpu.VMEM((3, 8, 128), f32),
            pltpu.VMEM((4, 8, 80, 128), jnp.bfloat16),
            pltpu.SemaphoreType.DMA((32,)),
            pltpu.SemaphoreType.DMA((32,)),
        ],
        compiler_params=pltpu.CompilerParams(collective_id=1, has_side_effects=True),
    )(g)


def shards(queries, keys, values, feat_q, key_feature_weights, doc_start):
    rows, heads, width = queries.shape
    groups = keys.shape[1]
    tokens = rows * lax.axis_size("seq")
    kv = jnp.concatenate([keys, values], axis=1).transpose(1, 0, 2).reshape(2 * groups * rows, width)
    gathered = gather(kv).reshape(64, 2 * groups, rows, width)
    teacher, student, g = run(
        doc_start,
        gathered,
        queries,
        feat_q.transpose(0, 2, 1),
        key_feature_weights.transpose(0, 2, 1),
        tokens,
        SPAN,
        TILE,
    )
    entries = (heads + groups) * lax.axis_size("head") * width * 64
    gq, gk = reduce(g.reshape(4, 8, 72, 128), entries)
    return teacher, student, gq.transpose(0, 2, 1), gk.transpose(0, 2, 1)


def solution(mesh):
    placed = (
        P("seq", "head", None),
        P("seq", "head", None),
        P("seq", "head", None),
        P("head", None, None),
        P("head", None, None),
        P("seq"),
    )
    return jax.shard_map(
        shards,
        mesh=mesh,
        in_specs=placed,
        out_specs=placed[:2] + placed[3:5],
        check_vma=False,
    )
```

```python
import functools, math
import jax, jax.numpy as jnp
from jax import lax
from jax.experimental import pallas as pl
from jax.experimental.pallas import tpu as pltpu
from jax.sharding import PartitionSpec as P

F32, BF16 = jnp.float32, jnp.bfloat16
NN = (((1,), (0,)), ((), ()))
NT = (((1,), (1,)), ((), ()))
TN = (((0,), (0,)), ((), ()))
LOW = -1e30
BATCH = 16
SPAN, TILE = 1024, 128
PASS = (3, 3, 3, 3, 2, 3, 3, 2, 2)


def dot(a, b, dims=NN):
    return lax.dot_general(a, b, dims, preferred_element_type=F32)


def halves(x):
    hi = x.astype(BF16)
    return hi, (x - hi.astype(F32)).astype(BF16)


def soft(x):
    e = jnp.exp(-jnp.abs(x))
    one = 1.0 + e
    log = jnp.where(e < 1e-3, e * (1.0 - e * (0.5 - e * (1.0 / 3.0))), jnp.log(one))
    return e, log, 1.0 / one


def soft_lanes(x):
    e, log, inverse = soft(x)
    return jnp.maximum(x, 0.0) + log, jnp.where(x >= 0.0, 1.0, e) * inverse


def soft_rows(x):
    e, log, inverse = soft(x)
    other = e * inverse
    feat = jnp.concatenate([jnp.maximum(x, 0.0) + log, jnp.maximum(-x, 0.0) + log], axis=0)
    slope = jnp.concatenate(
        [jnp.where(x >= 0.0, inverse, other), jnp.where(x >= 0.0, other, inverse)], axis=0
    )
    return feat, slope


def stacked(a, b):
    both = dot(jnp.concatenate(a, axis=0), b)
    return both[: both.shape[0] // 2] + both[both.shape[0] // 2 :]


def dots(passes, a, b, dims=NN):
    out = dot(a[0], b[0], dims)
    if passes > 1:
        out = out + dot(a[1], b[0], dims)
    if passes > 2:
        out = out + dot(a[0], b[1], dims)
    return out


def signed(weight):
    return jnp.concatenate([weight, -weight], axis=0)


def compute(span, tile, tokens, pos, doc_ref, k_ref, v_ref, q_ref, wq_ref, wk_ref,
            t_ref, s_ref, g_ref,
            top, acc, sig, state, dstate, dkey, wide, q_s):
    slots = span // 128
    heads = q_ref.shape[1]
    mine, first = lax.axis_index("seq"), pos[0]
    begin = mine * 128
    first_slot = first // 128
    blocks = (mine - first_slot + slots - 1) // slots
    logit = math.log2(math.e) / math.sqrt(128)
    lanes = lax.broadcasted_iota(jnp.int32, (1, span), 1)
    ones = jnp.ones((span, 128), BF16)

    def loads(i):
        at = jnp.minimum(first_slot + i * slots, 64 - slots)
        k = k_ref[pl.ds(at, slots), 0].reshape(span, 128)
        v = v_ref[pl.ds(at, slots), 0].reshape(span, 128)
        key = at * 128 + lanes
        live = (key >= jnp.maximum(first, (first_slot + i * slots) * 128)) & (key < begin)
        return k, jnp.concatenate([v, ones], axis=1), live

    top[...] = jnp.full_like(top, LOW)
    acc[...] = jnp.zeros_like(acc)
    state[...] = jnp.zeros_like(state)
    dstate[...] = jnp.zeros_like(dstate)
    dkey[...] = jnp.zeros_like(dkey)
    wkt = jnp.concatenate(halves(wk_ref[0]), axis=1)
    wide[...] = q_ref[...].astype(F32)
    for h in range(heads):
        q_s[h] = wide[:, h, :].astype(BF16)

    def softmax_step(rows, raw, bias, v2):
        if bias is not None:
            raw = raw + bias
        old = top[rows, :]
        new = jnp.maximum(old, jnp.max(raw, axis=1, keepdims=True))
        base = new * logit
        weight = jnp.exp2(raw * logit - base[:, :1]).astype(BF16)
        shrink = jnp.exp2(old * logit - base)
        top[rows, :] = new
        acc[rows, :] = acc[rows, :] * jnp.concatenate([shrink, shrink], axis=1) + dot(weight, v2)

    def scores(r, k):
        q = q_s[r * (tile // 128) : (r + 1) * (tile // 128)].reshape(tile, 128)
        return dot(q, k, NT)

    def attend(k, v2, bias):
        count = heads * 128 // tile
        ahead = scores(0, k)
        for r in range(count):
            raw = ahead
            if r + 1 < count:
                ahead = scores(r + 1, k)
            softmax_step(slice(r * tile, (r + 1) * tile), raw, bias, v2)

    def prefix(i, _):
        k, v2, live = loads(i)
        feat, slope = soft_rows(dot(wkt, jnp.concatenate([k, k], axis=1), NT))
        feat = jnp.where(live, feat, 0.0)
        sig[i] = jnp.where(live, slope, 0.0)
        state[...] += stacked(halves(feat), v2)
        edge = (i == 0) | (i == blocks - 1)

        @pl.when(edge)
        def _():
            attend(k, v2, jnp.where(live, 0.0, LOW))

        @pl.when(jnp.logical_not(edge))
        def _():
            attend(k, v2, None)

        return 0

    lax.fori_loop(0, blocks, prefix, 0)

    doc = jnp.broadcast_to(doc_ref[...], (128, 128)).T
    at_s = lax.broadcasted_iota(jnp.int32, (128, 128), 1)
    at_t = lax.broadcasted_iota(jnp.int32, (128, 128), 0)
    allowed = (at_s <= at_t) & (at_s + begin >= doc)

    def spread(x):
        return jnp.concatenate([x] * BATCH, axis=0)

    match = spread((doc == first).astype(F32))
    match2 = jnp.concatenate([match, match], axis=1)
    bias = spread(jnp.where(allowed, 0.0, LOW))
    keep = spread(jnp.where(allowed, 1.0, 0.0))
    k = k_ref[mine, 0]
    v2 = jnp.concatenate([v_ref[mine, 0], ones[:128]], axis=1)
    kk = jnp.concatenate([k, k], axis=1)
    kf = halves(soft_lanes(dot(kk, signed(wkt), NT))[0])
    sh, sl = halves(state[...])
    bh = jnp.concatenate([v2, sh], axis=0)
    bl = jnp.concatenate([jnp.zeros_like(v2), sl], axis=0)
    full = BATCH * 128

    def some(b, _):
        h0 = b * BATCH
        rows = pl.ds(pl.multiple_of(b * full, full), full)
        q = q_s[pl.ds(h0, BATCH)].reshape(full, 128)
        top[rows, :] = jnp.where(match > 0.0, top[rows, :], LOW)
        acc[rows, :] = acc[rows, :] * match2
        softmax_step(rows, dot(q, k, NT), bias, v2)
        total = acc[rows, :]
        teacher = (total[:, :128] / total[:, 128:]).astype(BF16)
        for j in range(BATCH):
            wide[:, h0 + j, :] = teacher[j * 128 : (j + 1) * 128].astype(F32)
        both = []
        for j in range(BATCH):
            wq2 = signed(jnp.concatenate(halves(wq_ref[h0 + j]), axis=1))
            qj = q_s[h0 + j]
            both.append(dot(jnp.concatenate([qj, qj], axis=1), wq2, NT))
        feat, slope = soft_lanes(jnp.concatenate(both, axis=0))
        fs = halves(feat)
        sim = dots(PASS[0], fs, kf, NT) * keep
        a = halves(jnp.concatenate([sim, feat * match], axis=1))
        out = dots(PASS[1], a, (bh, bl))
        inverse = 1.0 / out[:, 128:]
        student = out[:, :128] * inverse
        for j in range(BATCH):
            s_ref[:, h0 + j, :] = student[j * 128 : (j + 1) * 128]
        tangent = (student - teacher.astype(F32)) * (inverse * (1.0 / math.sqrt(tokens)))
        loss = -jnp.sum(tangent * student, axis=1, keepdims=True) * (1.0 / 128.0)
        d = jnp.concatenate([tangent, jnp.broadcast_to(loss, (full, 128))], axis=1)
        da = dots(PASS[2], halves(d), (bh, bl), NT)
        dsim = halves(da[:, :128] * keep)
        dfeat = dots(PASS[3], dsim, kf) + da[:, 128:] * match
        dp = halves(dfeat * slope)
        for j in range(BATCH):
            part = slice(j * 128, (j + 1) * 128)
            gt = dots(PASS[4], (dp[0][part], dp[1][part]), (q_s[h0 + j],), TN)
            g_ref[h0 + j, 0:64] = gt[:64] - gt[64:]
        dkey[...] += dots(PASS[5], fs, dsim, TN)
        dstate[...] += dots(PASS[6], fs, halves(d * match2), TN)
        return 0

    for b in range(heads // BATCH):
        some(b, 0)
    t_ref[...] = wide[...].astype(BF16)

    _, slope = soft_rows(dot(wkt, kk, NT))
    state[:, :128] = stacked(halves(dkey[...] * slope), k)
    ds = jnp.concatenate(halves(dstate[...]), axis=0)

    def pull(i, _):
        k, v2, _ = loads(i)
        dk = dot(ds, v2, NT)
        state[:, :128] += stacked(halves((dk[:128] + dk[128:]) * sig[i]), k)
        return 0

    lax.fori_loop(0, blocks, pull, 0)
    gk = state[:64, :128] - state[64:, :128]
    pad = jnp.zeros((4, 128), F32)
    for j in range(heads):
        g_ref[j, 64:72] = jnp.concatenate([gk[4 * j : 4 * j + 4], pad], axis=0)


def run(doc, kv, q, wq, wk, tokens, span, tile):
    groups = wk.shape[0]
    heads = q.shape[1] // groups
    spec = pl.BlockSpec
    return pl.pallas_call(
        functools.partial(compute, span, tile, tokens),
        out_shape=(
            jax.ShapeDtypeStruct(q.shape, BF16),
            jax.ShapeDtypeStruct(q.shape, F32),
            jax.ShapeDtypeStruct((q.shape[1], 72, 128), F32),
        ),
        grid=(groups,),
        in_specs=[
            spec(memory_space=pltpu.SMEM),
            spec((1, 128), lambda g: (0, 0)),
            spec((64, 1, 128, 128), lambda g: (0, g, 0, 0)),
            spec((64, 1, 128, 128), lambda g: (0, g + groups, 0, 0)),
            spec((128, heads, 128), lambda g: (0, g, 0)),
            spec((heads, 64, 128), lambda g: (g, 0, 0)),
            spec((1, 64, 128), lambda g: (g, 0, 0)),
        ],
        out_specs=(
            spec((128, heads, 128), lambda g: (0, g, 0)),
            spec((128, heads, 128), lambda g: (0, g, 0)),
            spec((heads, 72, 128), lambda g: (g, 0, 0)),
        ),
        scratch_shapes=[
            pltpu.VMEM((heads * 128, 128), F32),
            pltpu.VMEM((heads * 128, 256), F32),
            pltpu.VMEM((64 * 128 // span, 128, span), F32),
            pltpu.VMEM((128, 256), F32),
            pltpu.VMEM((128, 256), F32),
            pltpu.VMEM((128, 128), F32),
            pltpu.VMEM((128, heads, 128), F32),
            pltpu.VMEM((heads, 128, 128), BF16),
        ],
        compiler_params=pltpu.CompilerParams(
            dimension_semantics=("arbitrary",), vmem_limit_bytes=58 * 2**20
        ),
    )(doc, doc.reshape(1, 128), kv, kv, q, wq, wk)


MESH = pl.DeviceIdType.MESH


def place():
    at = lax.axis_index("seq")
    return at // 16, (at // 2) % 8, at % 2


def seq_of(y, z, x):
    return {"seq": ((y + 4) % 4 * 8 + (z + 8) % 8) * 2 + x}


def greet(peers):
    barrier = pltpu.get_barrier_semaphore()
    for peer in peers:
        pl.semaphore_signal(barrier, inc=1, device_id=peer, device_id_type=MESH)
    pl.semaphore_wait(barrier, len(peers))


class Copies:
    def __init__(self, out_sem, in_sem):
        self.sems, self.all = (out_sem, in_sem), []

    def __call__(self, src, dst, peer):
        n = len(self.all)
        copy = pltpu.make_async_remote_copy(
            src_ref=src,
            dst_ref=dst,
            send_sem=self.sems[0].at[n],
            recv_sem=self.sems[1].at[n],
            device_id=peer,
            device_id_type=MESH,
        )
        copy.start()
        self.all.append(copy)
        return copy

    def finish(self):
        for copy in self.all:
            copy.wait_send()


PART_A, PART_B, PART_C = (0, 96, 176), (176, 256, 320), (320, 416, 512)


def gather_kernel(own, out, out_sem, in_sem, own_sem):
    y, z, x = place()
    greet(
        [seq_of(y, z, 1 - x)]
        + [seq_of(y + k, z, x) for k in (1, -1)]
        + [seq_of(y, z + k, x) for k in (1, -1)]
    )
    send = Copies(out_sem, in_sem)

    def ring(part, region, axis, source=None):
        size = 8 if axis == "z" else 4
        here = z if axis == "z" else y

        def toward(k):
            return seq_of(y, z + k, x) if axis == "z" else seq_of(y + k, z, x)

        def rows(a, b):
            return pl.ds(part[a], part[b] - part[a])

        for step in range(1, size // 2 + 1):
            last = step == size // 2
            cuts = ((0, 1), (1, 2)) if last else ((0, 2), (0, 2))
            back, fore = (here + size - step + 1) % size, (here + step - 1) % size
            pair = []
            for at, cut, k in ((back, cuts[0], 1), (fore, cuts[1], -1)):
                target = region(at, rows(*cut))
                from_here = source(rows(*cut)) if source is not None and step == 1 else target
                pair.append(send(from_here, target, toward(k)))
            yield
            for copy in pair:
                copy.wait_recv()

    keep = pltpu.make_async_copy(own, out.at[y, z, x], own_sem)
    keep.start()
    rows_c = pl.ds(PART_C[0], PART_C[2] - PART_C[0])
    across = seq_of(y, z, 1 - x)
    first = pl.ds(0, PART_C[0])
    cz = ring(PART_C, lambda i, r: out.at[y, i, x, r], "z", lambda r: own.at[r])
    ay = ring(PART_A, lambda i, r: out.at[i, z, :, r], "y")
    bz = ring(PART_B, lambda i, r: out.at[y, i, :, r], "z")
    az = ring(PART_A, lambda i, r: out.at[:, i, :, r], "z")
    cy = ring(PART_C, lambda i, r: out.at[i, :, x, r], "y")
    by = ring(PART_B, lambda i, r: out.at[i, :, :, r], "y")
    waits = []

    def over(i):
        region = out.at[i, :, x, rows_c]
        waits.append(send(region, region, across))

    def go(*streams):
        for stream in streams:
            next(stream, None)

    go(cz)
    cross = send(own.at[first], out.at[y, z, x, first], across)
    keep.wait()
    go(cz)
    cross.wait_recv()
    go(ay, bz, cz, ay, cz, ay, bz, cz, cy)
    over(y)
    go(az, bz, cy)
    over((y + 3) % 4)
    over((y + 1) % 4)
    go(bz, az, bz, by, az, cy)
    over((y + 2) % 4)
    go(by, az, by, az)
    for copy in waits:
        copy.wait_recv()
    send.finish()


def gather(own):
    return pl.pallas_call(
        gather_kernel,
        out_shape=jax.ShapeDtypeStruct((4, 8, 2) + own.shape, own.dtype),
        in_specs=[pl.BlockSpec(memory_space=pltpu.VMEM)],
        out_specs=pl.BlockSpec(memory_space=pl.ANY),
        scratch_shapes=[
            pltpu.SemaphoreType.DMA((48,)),
            pltpu.SemaphoreType.DMA((48,)),
            pltpu.SemaphoreType.DMA,
        ],
        compiler_params=pltpu.CompilerParams(collective_id=0, has_side_effects=True),
    )(own)


def reduce_kernel(entries, g, out_q, out_k, far, near, acc, mid, zin, piece, xin, sq, sqin, full, out_sem, in_sem):
    y, z, x = place()
    head = lax.axis_index("head")
    peers_z = [seq_of(y, z + k, x) for k in range(1, 8)]
    peers_h = [{"head": (head + k) % 4} for k in range(1, 4)]
    up, down, across = seq_of(y + 1, z, x), seq_of(y - 1, z, x), seq_of(y, z, 1 - x)
    greet([up, down, across] + peers_z + peers_h)
    send = Copies(out_sem, in_sem)
    lo, hi = pl.ds(0, 4), pl.ds(4, 4)
    opposite, above, below = (y + 2) % 4, (y + 1) % 4, (y + 3) % 4
    far_up = send(g.at[opposite, lo], far.at[0], up)
    far_down = send(g.at[opposite, hi], far.at[1], down)
    near_up = send(g.at[above, hi], near.at[0], up)
    near_down = send(g.at[below, lo], near.at[1], down)
    far_up.wait_recv()
    acc[0] = g[above, lo] + far[0]
    acc_up = send(acc.at[0], near.at[2], up)
    far_down.wait_recv()
    acc[1] = g[below, hi] + far[1]
    acc_down = send(acc.at[1], near.at[3], down)
    near_up.wait_recv()
    near_down.wait_recv()
    acc_up.wait_recv()
    acc_down.wait_recv()
    mid[lo] = g[y, lo] + near[1] + near[2]
    mid[hi] = g[y, hi] + near[0] + near[3]
    parts = [send(mid.at[(z + k) % 8], zin.at[k - 1], peers_z[k - 1]) for k in range(1, 8)]
    total = mid[z]
    for k, part in enumerate(parts):
        part.wait_recv()
        total = total + zin[k]
    piece[...] = total
    swap = send(piece, xin, across)
    swap.wait_recv()
    total = total + xin[...]
    squares = total[0:8] * total[0:8]
    for k in range(1, 9):
        squares = squares + total[8 * k : 8 * k + 8] * total[8 * k : 8 * k + 8]
    sq[...] = squares
    shares = [send(sq, sqin.at[k - 1], peers_h[k - 1]) for k in range(1, 4)]
    full[y, z, 0:64] = total[0:64].astype(jnp.bfloat16)
    for k, share in enumerate(shares):
        share.wait_recv()
        squares = squares + sqin[k]
    squares = jnp.sum(squares, axis=0, keepdims=True)
    coarse = squares.astype(jnp.bfloat16).astype(jnp.float32)
    row = lax.broadcasted_iota(jnp.int32, (8, 128), 0)
    pair = jnp.where(row == 0, coarse, jnp.where(row == 1, squares - coarse, 0.0))
    full[y, z, 64:80] = jnp.concatenate([total[64:72], pair], axis=0).astype(jnp.bfloat16)
    shard = full.at[y, z]
    for part in [send(shard, shard, peer) for peer in peers_z]:
        part.wait_recv()
    slab = full.at[y]
    both = [send(slab, slab, up), send(slab, slab, down)]
    both[0].wait_recv()
    half = full.at[below, lo]
    last = [send(half, half, up)]
    both[1].wait_recv()
    half = full.at[above, hi]
    last.append(send(half, half, down))
    for copy in last:
        copy.wait_recv()
    ends = [full[k // 8, k % 8, 64:80].astype(jnp.float32) for k in range(32)]
    squares = ends[0][8:16]
    for end in ends[1:]:
        squares = squares + end[8:16]
    factor = 1.0 / jnp.sqrt(jnp.broadcast_to(jnp.sum(squares) * (1.0 / entries) + 1e-6, (64, 128)))
    for k, end in enumerate(ends):
        out_k[k // 16, 4 * (k % 16) : 4 * (k % 16) + 4] = end[0:4] * factor[0:4]

    def scale(k, _):
        out_q[k] = full[k // 8, k % 8, 0:64].astype(jnp.float32) * factor
        return 0

    lax.fori_loop(0, 32, scale, 0)
    send.finish()


def reduce(g, entries):
    f32 = jnp.float32
    return pl.pallas_call(
        functools.partial(reduce_kernel, entries),
        out_shape=(
            jax.ShapeDtypeStruct((32, 64, 128), f32),
            jax.ShapeDtypeStruct((2, 64, 128), f32),
        ),
        in_specs=[pl.BlockSpec(memory_space=pltpu.VMEM)],
        out_specs=(pl.BlockSpec(memory_space=pltpu.VMEM),) * 2,
        scratch_shapes=[
            pltpu.VMEM((2, 4, 72, 128), f32),
            pltpu.VMEM((4, 4, 72, 128), f32),
            pltpu.VMEM((2, 4, 72, 128), f32),
            pltpu.VMEM((8, 72, 128), f32),
            pltpu.VMEM((7, 72, 128), f32),
            pltpu.VMEM((72, 128), f32),
            pltpu.VMEM((72, 128), f32),
            pltpu.VMEM((8, 128), f32),
            pltpu.VMEM((3, 8, 128), f32),
            pltpu.VMEM((4, 8, 80, 128), jnp.bfloat16),
            pltpu.SemaphoreType.DMA((32,)),
            pltpu.SemaphoreType.DMA((32,)),
        ],
        compiler_params=pltpu.CompilerParams(collective_id=1, has_side_effects=True),
    )(g)


def shards(queries, keys, values, feat_q, key_feature_weights, doc_start):
    rows, heads, width = queries.shape
    groups = keys.shape[1]
    tokens = rows * lax.axis_size("seq")
    kv = jnp.concatenate([keys, values], axis=1).transpose(1, 0, 2).reshape(2 * groups * rows, width)
    gathered = gather(kv).reshape(64, 2 * groups, rows, width)
    teacher, student, g = run(
        doc_start,
        gathered,
        queries,
        feat_q.transpose(0, 2, 1),
        key_feature_weights.transpose(0, 2, 1),
        tokens,
        SPAN,
        TILE,
    )
    entries = (heads + groups) * lax.axis_size("head") * width * 64
    gq, gk = reduce(g.reshape(4, 8, 72, 128), entries)
    return teacher, student, gq.transpose(0, 2, 1), gk.transpose(0, 2, 1)


def solution(mesh):
    placed = (
        P("seq", "head", None),
        P("seq", "head", None),
        P("seq", "head", None),
        P("head", None, None),
        P("head", None, None),
        P("seq"),
    )
    return jax.shard_map(
        shards,
        mesh=mesh,
        in_specs=placed,
        out_specs=placed[:2] + placed[3:5],
        check_vma=False,
    )
```

```python
import functools, math
import jax, jax.numpy as jnp
from jax import lax
from jax.experimental import pallas as pl
from jax.experimental.pallas import tpu as pltpu
from jax.sharding import PartitionSpec as P

F32, BF16 = jnp.float32, jnp.bfloat16
NN = (((1,), (0,)), ((), ()))
NT = (((1,), (1,)), ((), ()))
TN = (((0,), (0,)), ((), ()))
LOW = -1e30
BATCH = 16
SPAN, TILE = 1024, 128
PASS = (3, 3, 3, 3, 2, 3, 3, 2, 2)


def dot(a, b, dims=NN):
    return lax.dot_general(a, b, dims, preferred_element_type=F32)


def halves(x):
    hi = x.astype(BF16)
    return hi, (x - hi.astype(F32)).astype(BF16)


def soft(x):
    e = jnp.exp(-jnp.abs(x))
    one = 1.0 + e
    log = jnp.where(e < 1e-3, e * (1.0 - e * (0.5 - e * (1.0 / 3.0))), jnp.log(one))
    return e, log, 1.0 / one


def soft_lanes(x):
    e, log, inverse = soft(x)
    return jnp.maximum(x, 0.0) + log, jnp.where(x >= 0.0, 1.0, e) * inverse


def soft_rows(x):
    e, log, inverse = soft(x)
    other = e * inverse
    feat = jnp.concatenate([jnp.maximum(x, 0.0) + log, jnp.maximum(-x, 0.0) + log], axis=0)
    slope = jnp.concatenate(
        [jnp.where(x >= 0.0, inverse, other), jnp.where(x >= 0.0, other, inverse)], axis=0
    )
    return feat, slope


def stacked(a, b):
    both = dot(jnp.concatenate(a, axis=0), b)
    return both[: both.shape[0] // 2] + both[both.shape[0] // 2 :]


def dots(passes, a, b, dims=NN):
    out = dot(a[0], b[0], dims)
    if passes > 1:
        out = out + dot(a[1], b[0], dims)
    if passes > 2:
        out = out + dot(a[0], b[1], dims)
    return out


def signed(weight):
    return jnp.concatenate([weight, -weight], axis=0)


def compute(span, tile, tokens, pos, doc_ref, k_ref, v_ref, q_ref, wq_ref, wk_ref,
            t_ref, s_ref, g_ref,
            top, acc, sig, state, dstate, dkey, wide, q_s):
    slots = span // 128
    heads = q_ref.shape[1]
    mine, first = lax.axis_index("seq"), pos[0]
    begin = mine * 128
    first_slot = first // 128
    whole = (mine - first_slot) // slots
    rest = (mine - first_slot) % slots
    blocks = whole + jnp.where(rest > slots // 2, 1, 0)
    short = (rest > 0) & (rest <= slots // 2)
    logit = math.log2(math.e) / math.sqrt(128)
    ones = jnp.ones((span, 128), BF16)

    def loads(i, size):
        at = jnp.minimum(first_slot + i * slots, 64 - size)
        k = k_ref[pl.ds(at, size), 0].reshape(size * 128, 128)
        v = v_ref[pl.ds(at, size), 0].reshape(size * 128, 128)
        key = at * 128 + lax.broadcasted_iota(jnp.int32, (1, size * 128), 1)
        live = (key >= jnp.maximum(first, (first_slot + i * slots) * 128)) & (key < begin)
        return k, jnp.concatenate([v, ones[: size * 128]], axis=1), live

    top[...] = jnp.full_like(top, LOW)
    acc[...] = jnp.zeros_like(acc)
    state[...] = jnp.zeros_like(state)
    dstate[...] = jnp.zeros_like(dstate)
    dkey[...] = jnp.zeros_like(dkey)
    wkt = jnp.concatenate(halves(wk_ref[0]), axis=1)
    wide[...] = q_ref[...].astype(F32)
    for h in range(heads):
        q_s[h] = wide[:, h, :].astype(BF16)

    def softmax_step(rows, raw, bias, v2):
        if bias is not None:
            raw = raw + bias
        old = top[rows, :]
        new = jnp.maximum(old, jnp.max(raw, axis=1, keepdims=True))
        base = new * logit
        weight = jnp.exp2(raw * logit - base[:, :1]).astype(BF16)
        shrink = jnp.exp2(old * logit - base)
        top[rows, :] = new
        acc[rows, :] = acc[rows, :] * jnp.concatenate([shrink, shrink], axis=1) + dot(weight, v2)

    def scores(r, k):
        q = q_s[r * (tile // 128) : (r + 1) * (tile // 128)].reshape(tile, 128)
        return dot(q, k, NT)

    def attend(k, v2, bias):
        count = heads * 128 // tile
        ahead = scores(0, k)
        for r in range(count):
            raw = ahead
            if r + 1 < count:
                ahead = scores(r + 1, k)
            softmax_step(slice(r * tile, (r + 1) * tile), raw, bias, v2)

    def learn(i, size):
        k, v2, live = loads(i, size)
        feat, slope = soft_rows(dot(wkt, jnp.concatenate([k, k], axis=1), NT))
        feat = jnp.where(live, feat, 0.0)
        sig[i, :, : size * 128] = jnp.where(live, slope, 0.0)
        state[...] += stacked(halves(feat), v2)
        return k, v2, jnp.where(live, 0.0, LOW)

    def prefix(i, _):
        k, v2, bias = learn(i, slots)
        edge = (i == 0) | (i == whole)

        @pl.when(edge)
        def _():
            attend(k, v2, bias)

        @pl.when(jnp.logical_not(edge))
        def _():
            attend(k, v2, None)

        return 0

    lax.fori_loop(0, blocks, prefix, 0)

    @pl.when(short)
    def _():
        attend(*learn(whole, slots // 2))

    doc = jnp.broadcast_to(doc_ref[...], (128, 128)).T
    at_s = lax.broadcasted_iota(jnp.int32, (128, 128), 1)
    at_t = lax.broadcasted_iota(jnp.int32, (128, 128), 0)
    allowed = (at_s <= at_t) & (at_s + begin >= doc)

    def spread(x):
        return jnp.concatenate([x] * BATCH, axis=0)

    match = spread((doc == first).astype(F32))
    match2 = jnp.concatenate([match, match], axis=1)
    bias = spread(jnp.where(allowed, 0.0, LOW))
    keep = spread(jnp.where(allowed, 1.0, 0.0))
    k = k_ref[mine, 0]
    v2 = jnp.concatenate([v_ref[mine, 0], ones[:128]], axis=1)
    kk = jnp.concatenate([k, k], axis=1)
    kf = halves(soft_lanes(dot(kk, signed(wkt), NT))[0])
    sh, sl = halves(state[...])
    bh = jnp.concatenate([v2, sh], axis=0)
    bl = jnp.concatenate([jnp.zeros_like(v2), sl], axis=0)
    full = BATCH * 128

    def some(b, _):
        h0 = b * BATCH
        rows = pl.ds(pl.multiple_of(b * full, full), full)
        q = q_s[pl.ds(h0, BATCH)].reshape(full, 128)
        top[rows, :] = jnp.where(match > 0.0, top[rows, :], LOW)
        acc[rows, :] = acc[rows, :] * match2
        softmax_step(rows, dot(q, k, NT), bias, v2)
        total = acc[rows, :]
        teacher = (total[:, :128] / total[:, 128:]).astype(BF16)
        for j in range(BATCH):
            wide[:, h0 + j, :] = teacher[j * 128 : (j + 1) * 128].astype(F32)
        both = []
        for j in range(BATCH):
            wq2 = signed(jnp.concatenate(halves(wq_ref[h0 + j]), axis=1))
            qj = q_s[h0 + j]
            both.append(dot(jnp.concatenate([qj, qj], axis=1), wq2, NT))
        feat, slope = soft_lanes(jnp.concatenate(both, axis=0))
        fs = halves(feat)
        sim = dots(PASS[0], fs, kf, NT) * keep
        a = halves(jnp.concatenate([sim, feat * match], axis=1))
        out = dots(PASS[1], a, (bh, bl))
        inverse = 1.0 / out[:, 128:]
        student = out[:, :128] * inverse
        for j in range(BATCH):
            s_ref[:, h0 + j, :] = student[j * 128 : (j + 1) * 128]
        tangent = (student - teacher.astype(F32)) * (inverse * (1.0 / math.sqrt(tokens)))
        loss = -jnp.sum(tangent * student, axis=1, keepdims=True) * (1.0 / 128.0)
        d = jnp.concatenate([tangent, jnp.broadcast_to(loss, (full, 128))], axis=1)
        da = dots(PASS[2], halves(d), (bh, bl), NT)
        dsim = halves(da[:, :128] * keep)
        dfeat = dots(PASS[3], dsim, kf) + da[:, 128:] * match
        dp = halves(dfeat * slope)
        for j in range(BATCH):
            part = slice(j * 128, (j + 1) * 128)
            gt = dots(PASS[4], (dp[0][part], dp[1][part]), (q_s[h0 + j],), TN)
            g_ref[h0 + j, 0:64] = gt[:64] - gt[64:]
        dkey[...] += dots(PASS[5], fs, dsim, TN)
        dstate[...] += dots(PASS[6], fs, halves(d * match2), TN)
        return 0

    for b in range(heads // BATCH):
        some(b, 0)
    t_ref[...] = wide[...].astype(BF16)

    _, slope = soft_rows(dot(wkt, kk, NT))
    state[:, :128] = stacked(halves(dkey[...] * slope), k)
    ds = jnp.concatenate(halves(dstate[...]), axis=0)

    def pull(i, size):
        k, v2, _ = loads(i, size)
        dk = dot(ds, v2, NT)
        slope = sig[i, :, : size * 128]
        state[:, :128] += stacked(halves((dk[:128] + dk[128:]) * slope), k)
        return 0

    lax.fori_loop(0, blocks, lambda i, _: pull(i, slots), 0)

    @pl.when(short)
    def _():
        pull(whole, slots // 2)

    gk = state[:64, :128] - state[64:, :128]
    pad = jnp.zeros((4, 128), F32)
    for j in range(heads):
        g_ref[j, 64:72] = jnp.concatenate([gk[4 * j : 4 * j + 4], pad], axis=0)


def run(doc, kv, q, wq, wk, tokens, span, tile):
    groups = wk.shape[0]
    heads = q.shape[1] // groups
    spec = pl.BlockSpec
    return pl.pallas_call(
        functools.partial(compute, span, tile, tokens),
        out_shape=(
            jax.ShapeDtypeStruct(q.shape, BF16),
            jax.ShapeDtypeStruct(q.shape, F32),
            jax.ShapeDtypeStruct((q.shape[1], 72, 128), F32),
        ),
        grid=(groups,),
        in_specs=[
            spec(memory_space=pltpu.SMEM),
            spec((1, 128), lambda g: (0, 0)),
            spec((64, 1, 128, 128), lambda g: (0, g, 0, 0)),
            spec((64, 1, 128, 128), lambda g: (0, g + groups, 0, 0)),
            spec((128, heads, 128), lambda g: (0, g, 0)),
            spec((heads, 64, 128), lambda g: (g, 0, 0)),
            spec((1, 64, 128), lambda g: (g, 0, 0)),
        ],
        out_specs=(
            spec((128, heads, 128), lambda g: (0, g, 0)),
            spec((128, heads, 128), lambda g: (0, g, 0)),
            spec((heads, 72, 128), lambda g: (g, 0, 0)),
        ),
        scratch_shapes=[
            pltpu.VMEM((heads * 128, 128), F32),
            pltpu.VMEM((heads * 128, 256), F32),
            pltpu.VMEM((64 * 128 // span, 128, span), F32),
            pltpu.VMEM((128, 256), F32),
            pltpu.VMEM((128, 256), F32),
            pltpu.VMEM((128, 128), F32),
            pltpu.VMEM((128, heads, 128), F32),
            pltpu.VMEM((heads, 128, 128), BF16),
        ],
        compiler_params=pltpu.CompilerParams(
            dimension_semantics=("arbitrary",), vmem_limit_bytes=58 * 2**20
        ),
    )(doc, doc.reshape(1, 128), kv, kv, q, wq, wk)


MESH = pl.DeviceIdType.MESH


def place():
    at = lax.axis_index("seq")
    return at // 16, (at // 2) % 8, at % 2


def seq_of(y, z, x):
    return {"seq": ((y + 4) % 4 * 8 + (z + 8) % 8) * 2 + x}


def greet(peers):
    barrier = pltpu.get_barrier_semaphore()
    for peer in peers:
        pl.semaphore_signal(barrier, inc=1, device_id=peer, device_id_type=MESH)
    pl.semaphore_wait(barrier, len(peers))


class Copies:
    def __init__(self, out_sem, in_sem):
        self.sems, self.all = (out_sem, in_sem), []

    def __call__(self, src, dst, peer):
        n = len(self.all)
        copy = pltpu.make_async_remote_copy(
            src_ref=src,
            dst_ref=dst,
            send_sem=self.sems[0].at[n],
            recv_sem=self.sems[1].at[n],
            device_id=peer,
            device_id_type=MESH,
        )
        copy.start()
        self.all.append(copy)
        return copy

    def finish(self):
        for copy in self.all:
            copy.wait_send()


PART_A, PART_B, PART_C = (0, 96, 176), (176, 256, 320), (320, 416, 512)


def gather_kernel(own, out, out_sem, in_sem, own_sem):
    y, z, x = place()
    greet(
        [seq_of(y, z, 1 - x)]
        + [seq_of(y + k, z, x) for k in (1, -1)]
        + [seq_of(y, z + k, x) for k in (1, -1)]
    )
    send = Copies(out_sem, in_sem)

    def ring(part, region, axis, source=None):
        size = 8 if axis == "z" else 4
        here = z if axis == "z" else y

        def toward(k):
            return seq_of(y, z + k, x) if axis == "z" else seq_of(y + k, z, x)

        def rows(a, b):
            return pl.ds(part[a], part[b] - part[a])

        for step in range(1, size // 2 + 1):
            last = step == size // 2
            cuts = ((0, 1), (1, 2)) if last else ((0, 2), (0, 2))
            back, fore = (here + size - step + 1) % size, (here + step - 1) % size
            pair = []
            for at, cut, k in ((back, cuts[0], 1), (fore, cuts[1], -1)):
                target = region(at, rows(*cut))
                from_here = source(rows(*cut)) if source is not None and step == 1 else target
                pair.append(send(from_here, target, toward(k)))
            yield
            for copy in pair:
                copy.wait_recv()

    keep = pltpu.make_async_copy(own, out.at[y, z, x], own_sem)
    keep.start()
    rows_c = pl.ds(PART_C[0], PART_C[2] - PART_C[0])
    across = seq_of(y, z, 1 - x)
    first = pl.ds(0, PART_C[0])
    cz = ring(PART_C, lambda i, r: out.at[y, i, x, r], "z", lambda r: own.at[r])
    ay = ring(PART_A, lambda i, r: out.at[i, z, :, r], "y")
    bz = ring(PART_B, lambda i, r: out.at[y, i, :, r], "z")
    az = ring(PART_A, lambda i, r: out.at[:, i, :, r], "z")
    cy = ring(PART_C, lambda i, r: out.at[i, :, x, r], "y")
    by = ring(PART_B, lambda i, r: out.at[i, :, :, r], "y")
    waits = []

    def over(i):
        region = out.at[i, :, x, rows_c]
        waits.append(send(region, region, across))

    def go(*streams):
        for stream in streams:
            next(stream, None)

    go(cz)
    cross = send(own.at[first], out.at[y, z, x, first], across)
    keep.wait()
    go(cz)
    cross.wait_recv()
    go(ay, bz, cz, ay, cz, ay, bz, cz, cy)
    over(y)
    go(az, bz, cy)
    over((y + 3) % 4)
    over((y + 1) % 4)
    go(bz, az, bz, by, az, cy)
    over((y + 2) % 4)
    go(by, az, by, az)
    for copy in waits:
        copy.wait_recv()
    send.finish()


def gather(own):
    return pl.pallas_call(
        gather_kernel,
        out_shape=jax.ShapeDtypeStruct((4, 8, 2) + own.shape, own.dtype),
        in_specs=[pl.BlockSpec(memory_space=pltpu.VMEM)],
        out_specs=pl.BlockSpec(memory_space=pl.ANY),
        scratch_shapes=[
            pltpu.SemaphoreType.DMA((48,)),
            pltpu.SemaphoreType.DMA((48,)),
            pltpu.SemaphoreType.DMA,
        ],
        compiler_params=pltpu.CompilerParams(collective_id=0, has_side_effects=True),
    )(own)


def reduce_kernel(entries, g, out_q, out_k, far, near, acc, mid, zin, piece, xin, sq, sqin, full, out_sem, in_sem):
    y, z, x = place()
    head = lax.axis_index("head")
    peers_z = [seq_of(y, z + k, x) for k in range(1, 8)]
    peers_h = [{"head": (head + k) % 4} for k in range(1, 4)]
    up, down, across = seq_of(y + 1, z, x), seq_of(y - 1, z, x), seq_of(y, z, 1 - x)
    greet([up, down, across] + peers_z + peers_h)
    send = Copies(out_sem, in_sem)
    lo, hi = pl.ds(0, 4), pl.ds(4, 4)
    opposite, above, below = (y + 2) % 4, (y + 1) % 4, (y + 3) % 4
    far_up = send(g.at[opposite, lo], far.at[0], up)
    far_down = send(g.at[opposite, hi], far.at[1], down)
    near_up = send(g.at[above, hi], near.at[0], up)
    near_down = send(g.at[below, lo], near.at[1], down)
    far_up.wait_recv()
    acc[0] = g[above, lo] + far[0]
    acc_up = send(acc.at[0], near.at[2], up)
    far_down.wait_recv()
    acc[1] = g[below, hi] + far[1]
    acc_down = send(acc.at[1], near.at[3], down)
    near_up.wait_recv()
    near_down.wait_recv()
    acc_up.wait_recv()
    acc_down.wait_recv()
    mid[lo] = g[y, lo] + near[1] + near[2]
    mid[hi] = g[y, hi] + near[0] + near[3]
    parts = [send(mid.at[(z + k) % 8], zin.at[k - 1], peers_z[k - 1]) for k in range(1, 8)]
    total = mid[z]
    for k, part in enumerate(parts):
        part.wait_recv()
        total = total + zin[k]
    piece[...] = total
    swap = send(piece, xin, across)
    swap.wait_recv()
    total = total + xin[...]
    squares = total[0:8] * total[0:8]
    for k in range(1, 9):
        squares = squares + total[8 * k : 8 * k + 8] * total[8 * k : 8 * k + 8]
    sq[...] = squares
    shares = [send(sq, sqin.at[k - 1], peers_h[k - 1]) for k in range(1, 4)]
    full[y, z, 0:64] = total[0:64].astype(jnp.bfloat16)
    body, end = full.at[y, z, pl.ds(0, 64)], full.at[y, z, pl.ds(64, 16)]
    parts = [send(body, body, peer) for peer in peers_z]
    for k, share in enumerate(shares):
        share.wait_recv()
        squares = squares + sqin[k]
    squares = jnp.sum(squares, axis=0, keepdims=True)
    coarse = squares.astype(jnp.bfloat16).astype(jnp.float32)
    row = lax.broadcasted_iota(jnp.int32, (8, 128), 0)
    pair = jnp.where(row == 0, coarse, jnp.where(row == 1, squares - coarse, 0.0))
    full[y, z, 64:80] = jnp.concatenate([total[64:72], pair], axis=0).astype(jnp.bfloat16)
    for part in parts + [send(end, end, peer) for peer in peers_z]:
        part.wait_recv()
    slab = full.at[y]
    both = [send(slab, slab, up), send(slab, slab, down)]
    both[0].wait_recv()
    half = full.at[below, lo]
    last = [send(half, half, up)]
    both[1].wait_recv()
    half = full.at[above, hi]
    last.append(send(half, half, down))
    for copy in last:
        copy.wait_recv()
    ends = [full[k // 8, k % 8, 64:80].astype(jnp.float32) for k in range(32)]
    squares = ends[0][8:16]
    for end in ends[1:]:
        squares = squares + end[8:16]
    factor = 1.0 / jnp.sqrt(jnp.broadcast_to(jnp.sum(squares) * (1.0 / entries) + 1e-6, (64, 128)))
    for k, end in enumerate(ends):
        out_k[k // 16, 4 * (k % 16) : 4 * (k % 16) + 4] = end[0:4] * factor[0:4]

    def scale(k, _):
        out_q[k] = full[k // 8, k % 8, 0:64].astype(jnp.float32) * factor
        return 0

    lax.fori_loop(0, 32, scale, 0)
    send.finish()


def reduce(g, entries):
    f32 = jnp.float32
    return pl.pallas_call(
        functools.partial(reduce_kernel, entries),
        out_shape=(
            jax.ShapeDtypeStruct((32, 64, 128), f32),
            jax.ShapeDtypeStruct((2, 64, 128), f32),
        ),
        in_specs=[pl.BlockSpec(memory_space=pltpu.VMEM)],
        out_specs=(pl.BlockSpec(memory_space=pltpu.VMEM),) * 2,
        scratch_shapes=[
            pltpu.VMEM((2, 4, 72, 128), f32),
            pltpu.VMEM((4, 4, 72, 128), f32),
            pltpu.VMEM((2, 4, 72, 128), f32),
            pltpu.VMEM((8, 72, 128), f32),
            pltpu.VMEM((7, 72, 128), f32),
            pltpu.VMEM((72, 128), f32),
            pltpu.VMEM((72, 128), f32),
            pltpu.VMEM((8, 128), f32),
            pltpu.VMEM((3, 8, 128), f32),
            pltpu.VMEM((4, 8, 80, 128), jnp.bfloat16),
            pltpu.SemaphoreType.DMA((40,)),
            pltpu.SemaphoreType.DMA((40,)),
        ],
        compiler_params=pltpu.CompilerParams(collective_id=1, has_side_effects=True),
    )(g)


def shards(queries, keys, values, feat_q, key_feature_weights, doc_start):
    rows, heads, width = queries.shape
    groups = keys.shape[1]
    tokens = rows * lax.axis_size("seq")
    kv = jnp.concatenate([keys, values], axis=1).transpose(1, 0, 2).reshape(2 * groups * rows, width)
    gathered = gather(kv).reshape(64, 2 * groups, rows, width)
    teacher, student, g = run(
        doc_start,
        gathered,
        queries,
        feat_q.transpose(0, 2, 1),
        key_feature_weights.transpose(0, 2, 1),
        tokens,
        SPAN,
        TILE,
    )
    entries = (heads + groups) * lax.axis_size("head") * width * 64
    gq, gk = reduce(g.reshape(4, 8, 72, 128), entries)
    return teacher, student, gq.transpose(0, 2, 1), gk.transpose(0, 2, 1)


def solution(mesh):
    placed = (
        P("seq", "head", None),
        P("seq", "head", None),
        P("seq", "head", None),
        P("head", None, None),
        P("head", None, None),
        P("seq"),
    )
    return jax.shard_map(
        shards,
        mesh=mesh,
        in_specs=placed,
        out_specs=placed[:2] + placed[3:5],
        check_vma=False,
    )
```
